128 devices in a mesh: pipe: 8 (over x_hi, y), expert: 16 (over z, x_lo, core).
Axes of the slice: x: 4 (x_hi: 2, x_lo: 2; x = x_hi * 2 + x_lo), y: 4, z: 4, core: 2. Of those that a mesh axis runs over, the one named last changes fastest.
Arguments:
- x_fwd: bfloat16 [16384, 1536], P(('pipe', 'expert')), may hold values from -6 to 6
- gate_fwd: float32 [16384, 6], P(('pipe', 'expert')), may hold values from 0.05 to 0.4
- route_fwd: int32 [16384, 6], P(('pipe', 'expert')), may hold values from 0 to 31, all different within a row; in each aligned block of 128 rows (0 to 127, 128 to 255, ...) at most 32 rows name the same one
- x_bwd: bfloat16 [16384, 1536], P(('pipe', 'expert')), may hold values from -6 to 6
- gate_bwd: float32 [16384, 6], P(('pipe', 'expert')), may hold values from 0.05 to 0.4
- route_bwd: int32 [16384, 6], P(('pipe', 'expert')), may hold values from 0 to 31, all different within a row; in each aligned block of 128 rows (0 to 127, 128 to 255, ...) at most 32 rows name the same one
- cotangent: bfloat16 [16384, 1536], P(('pipe', 'expert')), may hold values from -6 to 6
- norm_gain: float32 [1536], replicated, may hold values from 0.5 to 1.5
- w_gate_up: bfloat16 [8, 32, 1536, 1536], P('pipe', 'expert'), as said below
- w_down: bfloat16 [8, 32, 768, 1536], P('pipe', 'expert'), as said below
Outputs:
- y_fwd: bfloat16 [16384, 1536], P(('pipe', 'expert'))
- dx_bwd: bfloat16 [16384, 1536], P(('pipe', 'expert'))
- grad_gate_up: bfloat16 [8, 16, 1536, 1536], P('pipe', 'expert')
- grad_down: bfloat16 [8, 16, 768, 1536], P('pipe', 'expert')
The draws below stay inside these ranges and needn't reach their ends.
Inputs may be any that keep to these rules, and one draw needn't show every extreme that they name: `route_fwd`: each row names 6 different experts; in the 128 rows of one group no expert is named more than 32 times. `route_bwd`: each row names 6 different experts; in the 128 rows of one group no expert is named more than 32 times. w_gate_up[p] equals w_gate_up[7 - p]. w_down[p] equals w_down[7 - p].
All inputs are finite; a program needn't handle non-finite values.
Results may differ from the reference program's by a relative error of at most 0.0078.
Values may be sent and summed in bfloat16 or wider, within the bound.
A program may use at most 192 MiB of HBM per device.

```python
import math
import jax
import jax.numpy as jnp
import numpy as np
from jax import lax

D = 1536
FF = 768
TOP = 6
EXP_DEV = 2
TOK_DEV = 128
SECTIONS = 8
GROUPS = 16
EXPERTS = 32
CAP = 32
ROWS = 16384


def mirrored_weights(key, shape, fan_in):
    half_shape = (SECTIONS // 2,) + shape
    values = jax.random.normal(key, half_shape, jnp.float32)
    values = (values * fan_in ** (-0.5)).astype(jnp.bfloat16)
    return jnp.concatenate([values, values[::-1]], axis=0)


def draw_w_gate_up(key, part):
    return mirrored_weights(jax.random.fold_in(key, 11), (EXPERTS, D, 2 * FF), D)


def draw_w_down(key, part):
    return mirrored_weights(jax.random.fold_in(key, 23), (EXPERTS, FF, D), FF)


def block_scale(key, dims, split, low, top_value):
    def one(position, shards_of):
        draws = jax.random.uniform(jax.random.fold_in(jax.random.fold_in(key, 6), position), (shards_of,), jnp.float32, low / len(split), top_value / len(split))
        return jnp.repeat(jnp.exp(draws), dims[position] // shards_of).reshape((-1,) + (1,) * (len(dims) - position - 1))

    factor_of = one(*split[0])
    for cut in split[1:]:
        factor_of = factor_of * one(*cut)
    return factor_of


def shared_out(own_key, own, number, rows, number_of, top, most, skew):
    order = jax.random.permutation(own_key, number_of)
    packed, ordinary = load_shares(number_of, rows * top, most, skew, True), load_shares(number_of, rows * top, most, skew, False)
    places = jnp.arange(number_of)

    def named(tallies, rotation):
        used = int((tallies > 0).sum())
        fixed = max(1, used // 4)
        passed = fixed + (places - fixed + rotation * (used - fixed)) % max(1, number_of - fixed)
        return jnp.zeros((number_of,), jnp.int32).at[order[jnp.where(places < fixed, places, passed)]].set(jnp.asarray(tallies, jnp.int32))

    tallies = jnp.where(number % 4 == 0, named(packed, number // 4), named(ordinary, number - number // 4 - 1))
    mixed = jax.random.permutation(jax.random.fold_in(own, 3), number_of)
    source_of, sink = mixed[0:number_of // 2 * 2:2], mixed[1:number_of // 2 * 2:2]
    room = jnp.minimum(tallies[source_of] - 1, most - tallies[sink]) // 2
    room = jnp.where((source_of == order[0]) | (sink == order[0]) | (tallies[sink] == 0), 0, jnp.maximum(room, 0))
    passed = jax.random.randint(jax.random.fold_in(own, 4), (number_of // 2,), 0, 1 << 20) % (room + 1)
    tallies = tallies.at[source_of].add(-passed).at[sink].add(passed)
    members = jnp.searchsorted(jnp.cumsum(tallies), jnp.arange(rows * top), side="right").astype(jnp.int32)
    table = members.reshape(top, rows).T
    table = table[jax.random.permutation(jax.random.fold_in(own, 1), rows)]
    rotation = jax.random.randint(jax.random.fold_in(own, 2), (rows, 1), 0, top)
    return jnp.take_along_axis(table, (jnp.arange(top)[None, :] + rotation) % top, axis=1)


def load_shares(amount, total, limit, skew, full):
    portions = [(1 << 20) // math.isqrt(standing ** skew) + 1 for standing in range(1, amount + 1)]
    largest = limit if full else min(limit, max(-(-total // amount), total * portions[0] // sum(portions)))
    least = 1 if total - largest >= amount - 1 else 0
    counts, spare = [largest] + [least] * (amount - 1), total - largest - least * (amount - 1)
    while spare > 0:
        movable = [i for i in range(1, amount) if counts[i] < largest] or [i for i in range(1, amount) if counts[i] < limit]
        whole, left = sum([portions[i] for i in movable]), spare
        for i in movable:
            extra = min(limit - counts[i], max(1, left * portions[i] // whole), spare)
            counts[i] = counts[i] + extra
            spare = spare - extra
    return np.array(counts)


def gaussian(key, dims, scale, reach, shards=(), kind=jnp.bfloat16):
    loudness = block_scale(key, dims, shards, -0.22, 0.18) if shards else 1.0
    drawn = jax.random.normal(key, dims, jnp.float32) * scale * loudness
    return jnp.minimum(jnp.maximum(drawn, -reach), reach).astype(kind)


def setup_inputs(seed: int = 0) -> dict:
    seeds = jax.random.split(jax.random.key(seed), 11)
    x_fwd = gaussian(seeds[0], (ROWS, D), 1.0, 6.0, ((0, 128),))
    gate_fwd = jnp.clip(0.05 + 0.35 * jax.random.uniform(seeds[1], (ROWS, TOP), jnp.float32) ** block_scale(seeds[1], (ROWS, TOP), ((0, 128),), -0.2, 0.2), 0.05, 0.4)
    route_fwd_keys = jax.random.split(jax.random.fold_in(seeds[2], 1), ROWS // TOK_DEV)
    route_fwd_turns = jax.random.permutation(jax.random.fold_in(seeds[2], 3), ROWS // TOK_DEV)
    route_fwd = jax.vmap(lambda own, number: shared_out(jax.random.fold_in(seeds[2], 2), own, number, TOK_DEV, EXPERTS, TOP, CAP, 2))(route_fwd_keys, route_fwd_turns).reshape((ROWS, TOP))
    x_bwd = gaussian(seeds[3], (ROWS, D), 1.0, 6.0, ((0, 128),))
    gate_bwd = jnp.clip(0.05 + 0.35 * jax.random.uniform(seeds[4], (ROWS, TOP), jnp.float32) ** block_scale(seeds[4], (ROWS, TOP), ((0, 128),), -0.2, 0.2), 0.05, 0.4)
    route_bwd_keys = jax.random.split(jax.random.fold_in(seeds[5], 1), ROWS // TOK_DEV)
    route_bwd_turns = jax.random.permutation(jax.random.fold_in(seeds[5], 3), ROWS // TOK_DEV)
    route_bwd = jax.vmap(lambda own, number: shared_out(jax.random.fold_in(seeds[5], 2), own, number, TOK_DEV, EXPERTS, TOP, CAP, 2))(route_bwd_keys, route_bwd_turns).reshape((ROWS, TOP))
    cotangent = gaussian(seeds[6], (ROWS, D), 1.0, 6.0, ((0, 128),))
    norm_gain = jnp.clip(1.0 + 0.1 * jax.random.normal(seeds[7], (D,), jnp.float32), 0.5, 1.5)
    w_gate_up = draw_w_gate_up(jax.random.fold_in(seeds[10], 71), 0)
    w_down = draw_w_down(jax.random.fold_in(seeds[10], 71), 0)
    return dict(x_fwd=x_fwd, gate_fwd=gate_fwd, route_fwd=route_fwd, x_bwd=x_bwd, gate_bwd=gate_bwd, route_bwd=route_bwd, cotangent=cotangent, norm_gain=norm_gain, w_gate_up=w_gate_up, w_down=w_down)


norm_eps = 1e-06

def normalize(inputs):
    values = inputs.astype(jnp.float32)
    scale = lax.rsqrt(lax.optimization_barrier(jnp.mean(values * values, axis=-1, keepdims=True)) + norm_eps)
    return (values * scale, scale)

def destinations(routes, expert_count, capacity):
    flat_routes = routes.reshape(-1)
    onehot = (flat_routes[:, None] == jnp.arange(expert_count, dtype=jnp.int32)[None, :]).astype(jnp.int32)
    before = jnp.cumsum(onehot, axis=0) - onehot
    slot = lax.optimization_barrier(jnp.sum(before * onehot, axis=1))
    return (flat_routes * capacity + slot).astype(jnp.int32).reshape(routes.shape)

def expert_forward(inputs, weight_gu, weight_dn):
    hidden_units = weight_dn.shape[1]
    both_parts = jnp.einsum('secd,edf->secf', inputs.astype(jnp.float32), weight_gu.astype(jnp.float32))
    gate_pre = both_parts[..., :hidden_units]
    up_pre = both_parts[..., hidden_units:]
    hidden = (jax.nn.silu(gate_pre) * up_pre).astype(jnp.bfloat16)
    return jnp.einsum('secf,efd->secd', hidden.astype(jnp.float32), weight_dn.astype(jnp.float32)).astype(jnp.bfloat16)

def expert_backward(inputs, cot_rows, weight_gu, weight_dn):
    hidden_units = weight_dn.shape[1]
    inputs_f = inputs.astype(jnp.float32)
    cot_f = cot_rows.astype(jnp.float32)
    gu_f = weight_gu.astype(jnp.float32)
    both_parts = jnp.einsum('secd,edf->secf', inputs_f, gu_f)
    gate_pre = both_parts[..., :hidden_units]
    up_pre = both_parts[..., hidden_units:]
    squash = jax.nn.sigmoid(gate_pre)
    activated = gate_pre * squash
    hidden = (activated * up_pre).astype(jnp.bfloat16)
    back_hidden = jnp.einsum('secd,efd->secf', cot_f, weight_dn.astype(jnp.float32))
    d_gate = back_hidden * up_pre * squash * (1.0 + gate_pre * (1.0 - squash))
    d_up = back_hidden * activated
    d_both = jnp.concatenate([d_gate, d_up], axis=-1).astype(jnp.bfloat16)
    d_both_f = d_both.astype(jnp.float32)
    d_inputs = jnp.einsum('secf,edf->secd', d_both_f, gu_f).astype(jnp.bfloat16)
    grad_dn = jnp.einsum('secf,secd->efd', hidden.astype(jnp.float32), cot_f).astype(jnp.bfloat16)
    grad_gu = jnp.einsum('secd,secf->edf', inputs_f, d_both_f).astype(jnp.bfloat16)
    return (d_inputs, grad_gu, grad_dn)

def rank_pass(x_f, g_f, r_f, x_b, g_b, r_b, cot, gain, weight_gu, weight_dn):
    slot_total = EXPERTS * CAP
    buffer_shape = (GROUPS, EXPERTS, CAP, D)

    def dest_of(routes):
        return destinations(routes, EXPERTS, CAP)

    def place_rows(values, dest):
        flat_values = values.reshape(-1, values.shape[-1])
        return jnp.zeros((slot_total, values.shape[-1]), values.dtype).at[dest.reshape(-1)].set(flat_values)

    def pick_rows(back, dest):
        return back[dest]
    h_f = (normalize(x_f)[0] * gain).astype(jnp.bfloat16)
    dest_f = jax.vmap(dest_of)(r_f)
    rows_f = jnp.broadcast_to(h_f[:, :, None, :], (GROUPS, TOK_DEV, TOP, D))
    send_f = jax.vmap(place_rows)(rows_f, dest_f).reshape(buffer_shape)
    out_f = expert_forward(send_f, weight_gu, weight_dn).reshape(GROUPS, slot_total, D)
    picked = jax.vmap(pick_rows)(out_f, dest_f)
    y_rows = lax.optimization_barrier(jnp.sum(picked.astype(jnp.float32) * g_f[..., None], axis=2)).astype(jnp.bfloat16)
    x_hat, scale = normalize(x_b)
    h_b = (x_hat * gain).astype(jnp.bfloat16)
    c_b = (g_b[..., None] * cot.astype(jnp.float32)[:, :, None, :]).astype(jnp.bfloat16)
    dest_b = jax.vmap(dest_of)(r_b)
    rows_b = jnp.broadcast_to(h_b[:, :, None, :], (GROUPS, TOK_DEV, TOP, D))
    send_h = jax.vmap(place_rows)(rows_b, dest_b).reshape(buffer_shape)
    send_c = jax.vmap(place_rows)(c_b, dest_b).reshape(buffer_shape)
    d_inputs, grad_gu, grad_dn = expert_backward(send_h, send_c, weight_gu, weight_dn)
    back_dh = d_inputs.reshape(GROUPS, slot_total, D)
    dh_sum = lax.optimization_barrier(jnp.sum(jax.vmap(pick_rows)(back_dh, dest_b).astype(jnp.float32), axis=2))
    scaled_dh = gain * dh_sum
    dx_rows = (scale * (scaled_dh - x_hat * lax.optimization_barrier(jnp.mean(x_hat * scaled_dh, axis=-1, keepdims=True)))).astype(jnp.bfloat16)
    return (y_rows, dx_rows, grad_gu, grad_dn)

def reference(x_fwd, gate_fwd, route_fwd, x_bwd, gate_bwd, route_bwd, cotangent, norm_gain, w_gate_up, w_down):
    stacked = (x_fwd.reshape(SECTIONS, GROUPS, TOK_DEV, D), gate_fwd.reshape(SECTIONS, GROUPS, TOK_DEV, TOP), route_fwd.reshape(SECTIONS, GROUPS, TOK_DEV, TOP), x_bwd.reshape(SECTIONS, GROUPS, TOK_DEV, D), gate_bwd.reshape(SECTIONS, GROUPS, TOK_DEV, TOP), route_bwd.reshape(SECTIONS, GROUPS, TOK_DEV, TOP), cotangent.reshape(SECTIONS, GROUPS, TOK_DEV, D))
    half_local = EXP_DEV // 2

    def take_row(array, index):
        return lax.dynamic_index_in_dim(array, index, 0, keepdims=False)

    def run_rank(index):
        pieces = [take_row(array, index) for array in stacked]
        return rank_pass(*pieces, norm_gain, take_row(w_gate_up, index), take_row(w_down, index))

    def pair_pass(lower):
        mirror = (SECTIONS - 1 - lower).astype(jnp.int32)
        low_side = run_rank(lower)
        high_side = run_rank(mirror)
        sum_gu = (low_side[2].astype(jnp.float32) + high_side[2].astype(jnp.float32)).astype(jnp.bfloat16)
        sum_dn = (low_side[3].astype(jnp.float32) + high_side[3].astype(jnp.float32)).astype(jnp.bfloat16)
        sum_gu = sum_gu.reshape(GROUPS, EXP_DEV, D, 2 * FF)
        sum_dn = sum_dn.reshape(GROUPS, EXP_DEV, FF, D)
        return (low_side[0], low_side[1], high_side[0], high_side[1], sum_gu[:, :half_local].reshape(GROUPS * half_local, D, 2 * FF), sum_gu[:, half_local:].reshape(GROUPS * half_local, D, 2 * FF), sum_dn[:, :half_local].reshape(GROUPS * half_local, FF, D), sum_dn[:, half_local:].reshape(GROUPS * half_local, FF, D))
    results = lax.map(pair_pass, jnp.arange(SECTIONS // 2, dtype=jnp.int32))
    y_fwd = jnp.concatenate([results[0], results[2][::-1]], axis=0).reshape(ROWS, D)
    dx_bwd = jnp.concatenate([results[1], results[3][::-1]], axis=0).reshape(ROWS, D)
    grad_gate_up = jnp.concatenate([results[4], results[5][::-1]], axis=0)
    grad_down = jnp.concatenate([results[6], results[7][::-1]], axis=0)
    return (y_fwd, dx_bwd, grad_gate_up, grad_down)
```

```python
import jax
import jax.numpy as jnp
from jax import lax
from jax.sharding import PartitionSpec as P

norm_eps = 1e-06
bf16 = jnp.bfloat16
f32 = jnp.float32


def normalize(inputs):
    values = inputs.astype(f32)
    scale = lax.rsqrt(jnp.mean(values * values, axis=-1, keepdims=True) + norm_eps)
    return values * scale, scale


def dispatch_table(routes, gates, expert_count, capacity):
    names = routes[:, :, None] == jnp.arange(expert_count, dtype=jnp.int32)[None, None, :]
    chosen = jnp.any(names, axis=1)
    gate = jnp.sum(jnp.where(names, gates[:, :, None], 0.0), axis=1)
    tokens = routes.shape[0]
    earlier = jnp.tri(tokens, tokens, -1, dtype=bf16)
    slot = jnp.dot(earlier, chosen.astype(bf16), preferred_element_type=f32).astype(jnp.int32)
    slot = jnp.where(chosen, slot, -1)
    pick = slot.T[:, None, :] == jnp.arange(capacity, dtype=jnp.int32)[None, :, None]
    slot_gate = jnp.sum(jnp.where(pick, gate.T[:, None, :], 0.0), axis=-1)
    return pick.astype(bf16), slot_gate


def per_device(
    x_fwd, gate_fwd, route_fwd, x_bwd, gate_bwd, route_bwd, cotangent, norm_gain, w_gate_up, w_down
):
    group_count = lax.axis_size("expert")
    section_count = lax.axis_size("pipe")
    local_count = w_gate_up.shape[1]
    expert_count = local_count * group_count
    token_count, width = x_fwd.shape
    picks = route_fwd.shape[1]
    capacity = token_count * picks * 4 // (3 * expert_count)
    hidden_units = w_down.shape[2]
    section = lax.axis_index("pipe")
    upper = (section >= section_count // 2).astype(jnp.int32)
    weight_gu, weight_dn = w_gate_up[0], w_down[0]

    bwd_hat, bwd_scale = normalize(x_bwd)
    bwd_normed = (bwd_hat * norm_gain).astype(bf16)
    pick_b, slot_gate_b = dispatch_table(route_bwd, gate_bwd, expert_count, capacity)
    order = (2, group_count * capacity)

    def by_parity(pick):
        return (
            pick.reshape(group_count, local_count, capacity, token_count)
            .transpose(1, 0, 2, 3)
            .reshape(expert_count * capacity, token_count)
        )

    pick_bp = by_parity(pick_b)
    gate_bp = (
        slot_gate_b.reshape(group_count, local_count, capacity)
        .transpose(1, 0, 2)
        .reshape(expert_count * capacity)
    )
    send_h = jnp.dot(pick_bp, bwd_normed, preferred_element_type=f32).astype(bf16)
    send_c = (jnp.dot(pick_bp, cotangent, preferred_element_type=f32) * gate_bp[:, None]).astype(bf16)

    pairs = [
        [p * group_count + d for p in (low, section_count - 1 - low) for d in range(group_count)]
        for low in range(section_count // 2)
    ]

    def exchange_pair(value):
        value = value.reshape(expert_count, capacity, width)
        return lax.all_to_all(
            value, ("pipe", "expert"), split_axis=0, concat_axis=0, axis_index_groups=pairs, tiled=True
        )

    def exchange(value):
        return lax.all_to_all(value, "expert", split_axis=0, concat_axis=0, tiled=True)

    recv_h = exchange_pair(send_h).reshape(expert_count * capacity, width)
    recv_c = exchange_pair(send_c).reshape(expert_count * capacity, width)

    fwd_normed = (normalize(x_fwd)[0] * norm_gain).astype(bf16)
    pick_f, slot_gate_f = dispatch_table(route_fwd, gate_fwd, expert_count, capacity)
    pick_f = pick_f.reshape(expert_count * capacity, token_count)
    send_f = jnp.dot(pick_f, fwd_normed, preferred_element_type=f32).astype(bf16)
    recv_f = exchange(send_f.reshape(group_count, local_count, capacity, width))

    own_gu = lax.dynamic_index_in_dim(weight_gu, upper, 0, keepdims=False)
    own_dn = lax.dynamic_index_in_dim(weight_dn, upper, 0, keepdims=False)
    both = jnp.dot(recv_h, own_gu, preferred_element_type=f32)
    gate_pre, up_pre = both[:, :hidden_units], both[:, hidden_units:]
    squash = jax.nn.sigmoid(gate_pre)
    activated = gate_pre * squash
    hidden = (activated * up_pre).astype(bf16)
    back_hidden = lax.dot_general(
        recv_c, own_dn, (((1,), (1,)), ((), ())), preferred_element_type=f32
    )
    d_gate = back_hidden * up_pre * squash * (1.0 + gate_pre * (1.0 - squash))
    d_up = back_hidden * activated
    d_both = jnp.concatenate([d_gate, d_up], axis=-1).astype(bf16)
    d_inputs = lax.dot_general(
        d_both, own_gu, (((1,), (1,)), ((), ())), preferred_element_type=f32
    ).astype(bf16)
    back_dh = exchange_pair(d_inputs).reshape(expert_count * capacity, width)
    grad_dn = lax.dot_general(
        hidden, recv_c, (((0,), (0,)), ((), ())), preferred_element_type=f32
    ).astype(bf16)
    grad_gu = lax.dot_general(
        recv_h, d_both, (((0,), (0,)), ((), ())), preferred_element_type=f32
    ).astype(bf16)

    fwd_both = jnp.einsum("secd,edf->secf", recv_f, weight_gu, preferred_element_type=f32)
    fwd_hidden = (
        jax.nn.silu(fwd_both[..., :hidden_units]) * fwd_both[..., hidden_units:]
    ).astype(bf16)
    out_fwd = jnp.einsum(
        "secf,efd->secd", fwd_hidden, weight_dn, preferred_element_type=f32
    ).astype(bf16)
    back_fwd = exchange(out_fwd).reshape(expert_count * capacity, width)

    scaled = (back_fwd.astype(f32) * slot_gate_f.reshape(-1)[:, None]).astype(bf16)
    contract_slots = (((0,), (0,)), ((), ()))
    y_fwd = lax.dot_general(pick_f, scaled, contract_slots, preferred_element_type=f32).astype(bf16)
    dh_sum = lax.dot_general(pick_bp, back_dh, contract_slots, preferred_element_type=f32)
    scaled_dh = norm_gain * dh_sum
    dx_bwd = (
        bwd_scale * (scaled_dh - bwd_hat * jnp.mean(bwd_hat * scaled_dh, axis=-1, keepdims=True))
    ).astype(bf16)
    return y_fwd, dx_bwd, grad_gu[None, None], grad_dn[None, None]


def solution(mesh):
    rows = P(("pipe", "expert"), None)
    weights = P("pipe", "expert", None, None)
    return jax.shard_map(
        per_device,
        mesh=mesh,
        in_specs=(rows,) * 7 + (P(), weights, weights),
        out_specs=(rows, rows, weights, weights),
        check_vma=False,
    )
```

```python
import functools

import jax
import jax.numpy as jnp
from jax import lax
from jax.experimental import pallas as pl
from jax.experimental.pallas import tpu as pltpu
from jax.sharding import PartitionSpec as P

norm_eps = 1e-06
bf16 = jnp.bfloat16
f32 = jnp.float32
MESH = pl.DeviceIdType.MESH
CAP = 32
TILE = 256
PIECE = 8 * CAP
NT = (((1,), (1,)), ((), ()))


def normalize(inputs):
    values = inputs.astype(f32)
    scale = lax.rsqrt(jnp.mean(values * values, axis=-1, keepdims=True) + norm_eps)
    return values * scale, scale


def place():
    p, d = lax.axis_index("pipe"), lax.axis_index("expert")
    half = p // 4
    return p, half, d // 4, (d // 2) % 2, d % 2


def peer(sign, kz, kx, kc, kh):
    p, half, z, xl, c = place()
    to_half = (half + kh) % 2
    flip = (half + to_half) % 2
    to_p = p + flip * (7 - 2 * p)
    to_z = (z + sign * kz + 4) % 4
    return to_p, to_z * 4 + ((xl + kx) % 2) * 2 + (c + kc) % 2


def dot(a, b):
    return jnp.dot(a, b, preferred_element_type=f32)


def dot_nt(a, b):
    return lax.dot_general(a, b, NT, preferred_element_type=f32)


def kernel(
    send_f, send_h, send_c, w_gu, w_dn,
    back_f, back_dh, grad_gu, grad_dn,
    got_f, got_h, got_c, gu, dn, out_f, out_dh, hid_f, hid, dboth, lhs_t, gout,
    w_sem, own_sem, fs_sem, fr_sem, hs_sem, hr_sem, cs_sem, cr_sem, ds_sem, dr_sem, es_sem, er_sem,
    g_sem,
):
    width = got_h.shape[1]
    units = dn.shape[1]
    p, half, z, xl, c = place()

    own = [
        pltpu.make_async_copy(send_f.at[0, 0], got_f.at[0, pl.ds(0, CAP)], own_sem.at[0]),
        pltpu.make_async_copy(send_f.at[1, 0], got_f.at[1, pl.ds(0, CAP)], own_sem.at[1]),
        pltpu.make_async_copy(send_h.at[0], got_h.at[pl.ds(0, CAP)], own_sem.at[2]),
        pltpu.make_async_copy(send_c.at[0], got_c.at[pl.ds(0, CAP)], own_sem.at[3]),
    ]
    weights = [
        pltpu.make_async_copy(w_gu, gu, w_sem.at[0]),
        pltpu.make_async_copy(w_dn, dn, w_sem.at[1]),
    ]
    for copy in own + weights:
        copy.start()

    barrier = pltpu.get_barrier_semaphore()

    def greet(k, _):
        to = peer(1, k % 4, (k // 8) % 2, (k // 4) % 2, k // 16)
        pl.semaphore_signal(barrier, inc=1, device_id=to, device_id_type=MESH)
        return 0

    lax.fori_loop(1, 32, greet, 0)
    pl.semaphore_wait(barrier, 31)

    def remote(src, dst, ssem, rsem, to):
        return pltpu.make_async_remote_copy(
            src_ref=src, dst_ref=dst, send_sem=ssem, recv_sem=rsem, device_id=to, device_id_type=MESH
        )

    def send_fwd(a):
        def go(j, _):
            to = peer(1, j % 4, a, j // 4, 0)
            slot = a * 8 + j
            rows = pl.ds(slot * CAP, CAP)
            for e in range(2):
                remote(
                    send_f.at[e, slot], got_f.at[e, rows], fs_sem.at[a, e], fr_sem.at[a, e], to
                ).start()
            return 0

        lax.fori_loop(1 if a == 0 else 0, 8, go, 0)

    def send_bwd(q):
        def go(j, _):
            to = peer(1, j % 4, q // 2, q % 2, j // 4)
            slot = q * 8 + j
            rows = pl.ds(slot * CAP, CAP)
            remote(send_h.at[slot], got_h.at[rows], hs_sem.at[q], hr_sem.at[q], to).start()
            remote(send_c.at[slot], got_c.at[rows], cs_sem.at[q], cr_sem.at[q], to).start()
            return 0

        lax.fori_loop(1 if q == 0 else 0, 8, go, 0)

    def return_fwd(a, e):
        def go(j, _):
            to = peer(-1, j % 4, a, j // 4, 0)
            slot = a * 8 + j
            remote(
                out_f.at[e, pl.ds(slot * CAP, CAP)], back_f.at[e, slot],
                ds_sem.at[e], dr_sem.at[e], to,
            ).start()
            return 0

        lax.fori_loop(1 if a == 0 else 0, 8, go, 0)

    def return_bwd(q):
        def go(j, _):
            to = peer(-1, j % 4, q // 2, q % 2, j // 4)
            slot = q * 8 + j
            remote(
                out_dh.at[pl.ds(slot * CAP, CAP)], back_dh.at[slot], es_sem.at[0], er_sem.at[0], to
            ).start()
            return 0

        lax.fori_loop(1 if q == 0 else 0, 8, go, 0)

    def span(q):
        first = CAP if q == 0 else 0
        return pl.ds(q * PIECE + first, PIECE - first)

    def landed(dst, ssem, rsem):
        return remote(dst, dst, ssem, rsem, (p, d_self))

    d_self = z * 4 + xl * 2 + c

    send_fwd(0)
    send_fwd(1)
    send_bwd(0)

    def forward_piece(a, e):
        rows = pl.ds(a * PIECE, PIECE)

        def first(t, _):
            at = pl.multiple_of(t * TILE, TILE)
            x = got_f[e, rows, :]
            gate = dot(x, gu[e, :, pl.ds(at, TILE)])
            up = dot(x, gu[e, :, pl.ds(units + at, TILE)])
            hid_f[:, pl.ds(at, TILE)] = (gate * jax.nn.sigmoid(gate) * up).astype(bf16)
            return 0

        lax.fori_loop(0, units // TILE, first, 0)

        def second(t, _):
            cols = pl.ds(pl.multiple_of(t * TILE, TILE), TILE)
            out_f[e, rows, cols] = dot(hid_f[...], dn[e, :, cols]).astype(bf16)
            return 0

        lax.fori_loop(0, width // TILE, second, 0)

    def backward_chain(q):
        rows = pl.ds(q * PIECE, PIECE)

        def first(t, _):
            at = pl.multiple_of(t * TILE, TILE)
            cols = pl.ds(at, TILE)
            more = pl.ds(units + at, TILE)
            x = got_h[rows, :]
            gate = dot(x, gu[half, :, cols])
            up = dot(x, gu[half, :, more])
            back = dot_nt(got_c[rows, :], dn[half, cols, :])
            squash = jax.nn.sigmoid(gate)
            active = gate * squash
            hid[rows, cols] = (active * up).astype(bf16)
            dboth[rows, cols] = (back * up * squash * (1.0 + gate * (1.0 - squash))).astype(bf16)
            dboth[rows, more] = (back * active).astype(bf16)
            return 0

        lax.fori_loop(0, units // TILE, first, 0)

        def second(t, _):
            cols = pl.ds(pl.multiple_of(t * TILE, TILE), TILE)
            out_dh[rows, cols] = dot_nt(dboth[rows, :], gu[half, cols, :]).astype(bf16)
            return 0

        lax.fori_loop(0, width // TILE, second, 0)

    for copy in own + weights:
        copy.wait()
    for a in range(2):
        for e in range(2):
            landed(got_f.at[e, span(a)], fs_sem.at[a, e], fr_sem.at[a, e]).wait_recv()
        send_bwd(1 + a)
        for e in range(2):
            forward_piece(a, e)
            return_fwd(a, e)
    send_bwd(3)
    for q in range(4):
        landed(got_h.at[span(q)], hs_sem.at[q], hr_sem.at[q]).wait_recv()
        landed(got_c.at[span(q)], cs_sem.at[q], cr_sem.at[q]).wait_recv()
        backward_chain(q)
        return_bwd(q)

    mine = [
        pltpu.make_async_copy(out_f.at[0, pl.ds(0, CAP)], back_f.at[0, 0], own_sem.at[0]),
        pltpu.make_async_copy(out_f.at[1, pl.ds(0, CAP)], back_f.at[1, 0], own_sem.at[1]),
        pltpu.make_async_copy(out_dh.at[pl.ds(0, CAP)], back_dh.at[0], own_sem.at[2]),
    ]
    for copy in mine:
        copy.start()

    def strips(lhs, rhs, count, dst, buf):
        def strip(m, _):
            at = pl.multiple_of(m * TILE, TILE)
            lhs_t[...] = lhs[:, pl.ds(at, TILE)].T

            def cols_of(t, _):
                cols = pl.ds(pl.multiple_of(t * TILE, TILE), TILE)
                gout[buf, :, cols] = dot(lhs_t[...], rhs[:, cols]).astype(bf16)
                return 0

            lax.fori_loop(0, width // TILE, cols_of, 0)
            copy = pltpu.make_async_copy(gout.at[buf], dst.at[pl.ds(at, TILE)], g_sem.at[buf])
            copy.start()
            copy.wait()
            return 0

        lax.fori_loop(0, count, strip, 0)

    strips(got_h, dboth, width // TILE, grad_gu, 0)
    strips(hid, got_c, units // TILE, grad_dn, 1)

    for a in range(2):
        for e in range(2):
            landed(got_f.at[e, span(a)], fs_sem.at[a, e], fr_sem.at[a, e]).wait_send()
    for q in range(4):
        landed(got_h.at[span(q)], hs_sem.at[q], hr_sem.at[q]).wait_send()
        landed(got_c.at[span(q)], cs_sem.at[q], cr_sem.at[q]).wait_send()
    for e in range(2):
        all_f = landed(back_f.at[e, pl.ds(1, 15)], ds_sem.at[e], dr_sem.at[e])
        all_f.wait_send()
        all_f.wait_recv()
    all_dh = landed(back_dh.at[pl.ds(1, 31)], es_sem.at[0], er_sem.at[0])
    all_dh.wait_send()
    all_dh.wait_recv()
    for copy in mine:
        copy.wait()


def dispatch_table(routes, gates, experts):
    names = routes[:, :, None] == experts[None, None, :]
    chosen = jnp.any(names, axis=1)
    gate = jnp.sum(jnp.where(names, gates[:, :, None], 0.0), axis=1)
    tokens = routes.shape[0]
    earlier = jnp.tri(tokens, tokens, -1, dtype=bf16)
    slot = dot(earlier, chosen.astype(bf16)).astype(jnp.int32)
    slot = jnp.where(chosen, slot, -1)
    pick = slot.T[:, None, :] == jnp.arange(CAP, dtype=jnp.int32)[None, :, None]
    slot_gate = jnp.sum(jnp.where(pick, gate.T[:, None, :], 0.0), axis=-1)
    return pick.astype(bf16).reshape(-1, tokens), slot_gate.reshape(-1, 1)


def per_device(
    x_fwd, gate_fwd, route_fwd, x_bwd, gate_bwd, route_bwd, cotangent, norm_gain, w_gate_up, w_down
):
    width = x_fwd.shape[1]
    units = w_down.shape[2]
    slots = 32

    k = jnp.arange(slots, dtype=jnp.int32)
    _, half, z, xl, c = place()
    near = ((z + k % 4) % 4) * 4
    d_b = near + ((xl + k // 16) % 2) * 2 + (c + (k // 8) % 2) % 2
    experts_b = 2 * d_b + (half + (k // 4) % 2) % 2
    j = k % 16
    d_f = ((z + j % 4) % 4) * 4 + ((xl + j // 8) % 2) * 2 + (c + (j // 4) % 2) % 2
    experts_f = 2 * d_f + k // 16

    bwd_hat, bwd_scale = normalize(x_bwd)
    bwd_normed = (bwd_hat * norm_gain).astype(bf16)
    pick_b, slot_gate_b = dispatch_table(route_bwd, gate_bwd, experts_b)
    send_h = dot(pick_b, bwd_normed).astype(bf16)
    send_c = (dot(pick_b, cotangent) * slot_gate_b).astype(bf16)
    fwd_normed = (normalize(x_fwd)[0] * norm_gain).astype(bf16)
    pick_f, slot_gate_f = dispatch_table(route_fwd, gate_fwd, experts_f)
    send_f = dot(pick_f, fwd_normed).astype(bf16)

    rows = slots * CAP
    anywhere = pl.BlockSpec(memory_space=pl.ANY)
    dma = pltpu.SemaphoreType.DMA
    back_f, back_dh, grad_gu, grad_dn = pl.pallas_call(
        kernel,
        out_shape=(
            jax.ShapeDtypeStruct((2, 16, CAP, width), bf16),
            jax.ShapeDtypeStruct((slots, CAP, width), bf16),
            jax.ShapeDtypeStruct((width, width), bf16),
            jax.ShapeDtypeStruct((units, width), bf16),
        ),
        in_specs=[anywhere] * 5,
        out_specs=(anywhere,) * 4,
        scratch_shapes=[
            pltpu.VMEM((2, rows // 2, width), bf16),
            pltpu.VMEM((rows, width), bf16),
            pltpu.VMEM((rows, width), bf16),
            pltpu.VMEM((2, width, width), bf16),
            pltpu.VMEM((2, units, width), bf16),
            pltpu.VMEM((2, rows // 2, width), bf16),
            pltpu.VMEM((rows, width), bf16),
            pltpu.VMEM((PIECE, units), bf16),
            pltpu.VMEM((rows, units), bf16),
            pltpu.VMEM((rows, width), bf16),
            pltpu.VMEM((TILE, rows), bf16),
            pltpu.VMEM((2, TILE, width), bf16),
            dma((2,)), dma((4,)), dma((2, 2)), dma((2, 2)),
            dma((4,)), dma((4,)), dma((4,)), dma((4,)),
            dma((2,)), dma((2,)), dma((1,)), dma((1,)), dma((2,)),
        ],
        compiler_params=pltpu.CompilerParams(
            collective_id=0, has_side_effects=True, vmem_limit_bytes=60 * 1024 * 1024
        ),
    )(
        send_f.reshape(2, 16, CAP, width),
        send_h.reshape(slots, CAP, width),
        send_c.reshape(slots, CAP, width),
        w_gate_up[0],
        w_down[0],
    )

    contract_slots = (((0,), (0,)), ((), ()))
    scaled = (back_f.reshape(rows, width).astype(f32) * slot_gate_f).astype(bf16)
    y_fwd = lax.dot_general(pick_f, scaled, contract_slots, preferred_element_type=f32).astype(bf16)
    dh_sum = lax.dot_general(
        pick_b, back_dh.reshape(rows, width), contract_slots, preferred_element_type=f32
    )
    scaled_dh = norm_gain * dh_sum
    dx_bwd = (
        bwd_scale * (scaled_dh - bwd_hat * jnp.mean(bwd_hat * scaled_dh, axis=-1, keepdims=True))
    ).astype(bf16)
    return y_fwd, dx_bwd, grad_gu[None, None], grad_dn[None, None]


def solution(mesh):
    rows = P(("pipe", "expert"), None)
    weights = P("pipe", "expert", None, None)
    return jax.shard_map(
        per_device,
        mesh=mesh,
        in_specs=(rows,) * 7 + (P(), weights, weights),
        out_specs=(rows, rows, weights, weights),
        check_vma=False,
    )
```

```python
import jax
import jax.numpy as jnp
from jax import lax
from jax.experimental import pallas as pl
from jax.experimental.pallas import tpu as pltpu
from jax.sharding import PartitionSpec as P

norm_eps = 1e-06
bf16 = jnp.bfloat16
f32 = jnp.float32
MESH = pl.DeviceIdType.MESH
CAP = 32
TILE = 256
WIDE = 512
PIECE = 8 * CAP
HALF = 16 * CAP
NT = (((1,), (1,)), ((), ()))


def place():
    p, d = lax.axis_index("pipe"), lax.axis_index("expert")
    return p, p // 4, d // 4, (d // 2) % 2, d % 2


def peer(sign, kz, kx, kc):
    p, _, z, xl, c = place()
    return p, ((z + sign * kz + 4) % 4) * 4 + ((xl + kx) % 2) * 2 + (c + kc) % 2


def mirror():
    p, _, z, xl, c = place()
    return 7 - p, z * 4 + (1 - xl) * 2 + c


def dot(a, b):
    return jnp.dot(a, b, preferred_element_type=f32)


def dot_nt(a, b):
    return lax.dot_general(a, b, NT, preferred_element_type=f32)


def loop(count, body):
    def step(i, _):
        body(i)
        return 0

    lax.fori_loop(0, count, step, 0)


def kernel(
    x_f, x_b, cot, gain, tab_f, tab_o, tab_m, w_gu, w_dn,
    y_out, dx_out, grad_gu, grad_dn,
    mx, mc, mtab, hf, hb, pick_f, pick_b, sent_f, sent_h, sent_c, got_f, got_h, got_c, gu, dn,
    out_f, out_dh, back_f, back_dh, hid_f, hid, dboth, lhs_t, gout, mine, theirs,
    w_sem, own_sem, ms_sem, mr_sem, fs_sem, fr_sem, hs_sem, hr_sem, cs_sem, cr_sem,
    ds_sem, dr_sem, es_sem, er_sem, ps_sem, pr_sem, g_sem,
):
    width = got_h.shape[1]
    units = dn.shape[1]
    p, half, z, xl, c = place()
    here = (p, z * 4 + xl * 2 + c)
    there = mirror()

    def remote(src, dst, ssem, rsem, to):
        return pltpu.make_async_remote_copy(
            src_ref=src, dst_ref=dst, send_sem=ssem, recv_sem=rsem, device_id=to, device_id_type=MESH
        )

    def landed(dst, ssem, rsem):
        return remote(dst, dst, ssem, rsem, here)

    barrier = pltpu.get_barrier_semaphore()
    pl.semaphore_signal(barrier, inc=1, device_id=there, device_id_type=MESH)

    def greet(k, _):
        to = peer(1, k % 4, k // 8, (k // 4) % 2)
        pl.semaphore_signal(barrier, inc=1, device_id=to, device_id_type=MESH)
        return 0

    lax.fori_loop(1, 16, greet, 0)

    weights = [
        pltpu.make_async_copy(w_gu, gu, w_sem.at[0]),
        pltpu.make_async_copy(w_dn, dn, w_sem.at[1]),
    ]
    for copy in weights:
        copy.start()

    def normalize(src, dst):
        def some(i):
            rows = pl.ds(pl.multiple_of(i * 32, 32), 32)
            v = src[rows, :].astype(f32)
            scale = lax.rsqrt(jnp.mean(v * v, axis=-1, keepdims=True) + norm_eps)
            dst[rows, :] = (v * scale * gain[...]).astype(bf16)

        loop(src.shape[0] // 32, some)

    def picks(table, first, dst, at):
        slots = table[0, first : first + 8, :]
        want = lax.broadcasted_iota(jnp.int32, (8, CAP, 128), 1).astype(f32)
        hit = jnp.where(slots[:, None, :] == want, 1.0, 0.0).reshape(PIECE, 128)
        dst[pl.ds(at, PIECE), :] = hit.astype(bf16)

    def slot_gates(table, first, pick, at):
        gates = table[1, first : first + 8, :]
        each = jnp.broadcast_to(gates[:, None, :], (8, CAP, 128)).reshape(PIECE, 128)
        return jnp.sum(pick[pl.ds(at, PIECE), :].astype(f32) * each, axis=1, keepdims=True)

    def spread(pick, at, src, dst, scale=None):
        def some(t):
            cols = pl.ds(pl.multiple_of(t * WIDE, WIDE), WIDE)
            rows = dot(pick[pl.ds(at, PIECE), :], src[:, cols])
            dst[:, cols] = (rows if scale is None else rows * scale).astype(bf16)

        loop(width // WIDE, some)

    def start_group(a, one):
        lax.fori_loop(1 if a == 0 else 0, 8, one, 0)

    def send_fwd(a):
        def go(j, _):
            to = peer(1, j % 4, a, j // 4)
            rows = pl.ds((a * 8 + j) * CAP, CAP)
            for e in range(2):
                remote(
                    sent_f.at[e, rows], got_f.at[e, rows], fs_sem.at[a, e], fr_sem.at[a, e], to
                ).start()
            return 0

        start_group(a, go)

    def send_bwd(r, a):
        def go(j, _):
            to = peer(1, j % 4, a, j // 4)
            rows = pl.ds(r * HALF + (a * 8 + j) * CAP, CAP)
            remote(sent_h.at[rows], got_h.at[rows], hs_sem.at[r, a], hr_sem.at[r, a], to).start()
            remote(sent_c.at[rows], got_c.at[rows], cs_sem.at[r, a], cr_sem.at[r, a], to).start()
            return 0

        start_group(a, go)

    def return_fwd(a, e):
        def go(j, _):
            to = peer(-1, j % 4, a, j // 4)
            rows = pl.ds((a * 8 + j) * CAP, CAP)
            remote(out_f.at[e, rows], back_f.at[e, rows], ds_sem.at[e], dr_sem.at[e], to).start()
            return 0

        start_group(a, go)

    def return_bwd(r, a):
        def go(j, _):
            to = peer(-1, j % 4, a, j // 4)
            rows = pl.ds(r * HALF + (a * 8 + j) * CAP, CAP)
            remote(out_dh.at[rows], back_dh.at[rows], es_sem.at[r], er_sem.at[r], to).start()
            return 0

        start_group(a, go)

    def span(base, a):
        skip = CAP if a == 0 else 0
        return pl.ds(base + a * PIECE + skip, PIECE - skip)

    def forward_piece(a, e):
        rows = pl.ds(a * PIECE, PIECE)

        def first(t):
            at = pl.multiple_of(t * TILE, TILE)
            x = got_f[e, rows, :]
            gate = dot(x, gu[e, :, pl.ds(at, TILE)])
            up = dot(x, gu[e, :, pl.ds(units + at, TILE)])
            hid_f[:, pl.ds(at, TILE)] = (gate * jax.nn.sigmoid(gate) * up).astype(bf16)

        loop(units // TILE, first)

        def second(t):
            cols = pl.ds(pl.multiple_of(t * TILE, TILE), TILE)
            out_f[e, rows, cols] = dot(hid_f[...], dn[e, :, cols]).astype(bf16)

        loop(width // TILE, second)

    def backward_chain(r, a):
        rows = pl.ds(r * HALF + a * PIECE, PIECE)

        def first(t):
            at = pl.multiple_of(t * TILE, TILE)
            cols = pl.ds(at, TILE)
            more = pl.ds(units + at, TILE)
            x = got_h[rows, :]
            gate = dot(x, gu[half, :, cols])
            up = dot(x, gu[half, :, more])
            back = dot_nt(got_c[rows, :], dn[half, cols, :])
            squash = jax.nn.sigmoid(gate)
            active = gate * squash
            hid[rows, cols] = (active * up).astype(bf16)
            dboth[rows, cols] = (back * up * squash * (1.0 + gate * (1.0 - squash))).astype(bf16)
            dboth[rows, more] = (back * active).astype(bf16)

        loop(units // TILE, first)

        def second(t):
            cols = pl.ds(pl.multiple_of(t * TILE, TILE), TILE)
            out_dh[rows, cols] = dot_nt(dboth[rows, :], gu[half, cols, :]).astype(bf16)

        loop(width // TILE, second)

    def strips(lhs, rhs, count, dst, buf):
        def strip(m):
            at = pl.multiple_of(m * TILE, TILE)
            lhs_t[...] = lhs[:, pl.ds(at, TILE)].T

            def cols_of(t):
                cols = pl.ds(pl.multiple_of(t * TILE, TILE), TILE)
                gout[buf, :, cols] = dot(lhs_t[...], rhs[:, cols]).astype(bf16)

            loop(width // TILE, cols_of)
            copy = pltpu.make_async_copy(gout.at[buf], dst.at[pl.ds(at, TILE)], g_sem.at[buf])
            copy.start()
            copy.wait()

        loop(count, strip)

    normalize(x_f, hf)
    for e in range(2):
        for a in range(2):
            at = e * HALF + a * PIECE
            picks(tab_f, e * 16 + a * 8, pick_f, at)
            spread(pick_f, at, hf, sent_f.at[e, pl.ds(a * PIECE, PIECE)])
    pl.semaphore_wait(barrier, 16)
    over = [
        remote(x_b, mx, ms_sem.at[0], mr_sem.at[0], there),
        remote(cot, mc, ms_sem.at[1], mr_sem.at[1], there),
        remote(tab_m, mtab, ms_sem.at[2], mr_sem.at[2], there),
    ]
    for copy in over:
        copy.start()
    send_fwd(0)
    send_fwd(1)
    own = [
        pltpu.make_async_copy(
            sent_f.at[e, pl.ds(0, CAP)], got_f.at[e, pl.ds(0, CAP)], own_sem.at[e]
        )
        for e in range(2)
    ]

    def dispatch(r, table, x_rows, c_rows):
        for a in range(2):
            at = r * HALF + a * PIECE
            picks(table, a * 8, pick_b, at)
            spread(pick_b, at, x_rows, sent_h.at[pl.ds(at, PIECE)])
            gates = slot_gates(table, a * 8, pick_b, at)
            spread(pick_b, at, c_rows, sent_c.at[pl.ds(at, PIECE)], gates)

    normalize(x_b, hb)
    dispatch(0, tab_o, hb, cot)
    for copy in over:
        copy.wait_recv()
    normalize(mx, hf)
    dispatch(1, mtab, hf, mc)
    send_bwd(1, 0)
    send_bwd(1, 1)
    for r in range(2):
        rows = pl.ds(r * HALF, CAP)
        own.append(pltpu.make_async_copy(sent_h.at[rows], got_h.at[rows], own_sem.at[2 + r]))
        own.append(pltpu.make_async_copy(sent_c.at[rows], got_c.at[rows], own_sem.at[4 + r]))
    for copy in own:
        copy.start()
    for copy in weights:
        copy.wait()
    for copy in own:
        copy.wait()

    for a in range(2):
        for e in range(2):
            landed(got_f.at[e, span(0, a)], fs_sem.at[a, e], fr_sem.at[a, e]).wait_recv()
        send_bwd(0, a)
        for e in range(2):
            forward_piece(a, e)
            return_fwd(a, e)
    for r in (1, 0):
        for a in range(2):
            where = span(r * HALF, a)
            landed(got_h.at[where], hs_sem.at[r, a], hr_sem.at[r, a]).wait_recv()
            landed(got_c.at[where], cs_sem.at[r, a], cr_sem.at[r, a]).wait_recv()
            backward_chain(r, a)
            return_bwd(r, a)

    home = [
        pltpu.make_async_copy(
            out_f.at[e, pl.ds(0, CAP)], back_f.at[e, pl.ds(0, CAP)], own_sem.at[e]
        )
        for e in range(2)
    ]
    for r in range(2):
        rows = pl.ds(r * HALF, CAP)
        home.append(pltpu.make_async_copy(out_dh.at[rows], back_dh.at[rows], own_sem.at[2 + r]))
    for copy in home:
        copy.start()
    for copy in home:
        copy.wait()

    strips(hid, got_c, units // TILE, grad_dn, 1)

    def returned(r):
        return landed(
            back_dh.at[pl.ds(r * HALF + CAP, HALF - CAP)], es_sem.at[r], er_sem.at[r]
        )

    def gathered(r, cols):
        total = None
        for a in range(2):
            rows = pl.ds(r * HALF + a * PIECE, PIECE)
            part = dot(pick_b[rows, :].T, back_dh[rows, cols])
            total = part if total is None else total + part
        return total

    returned(1).wait_recv()

    def sum_mirror(t):
        cols = pl.ds(pl.multiple_of(t * WIDE, WIDE), WIDE)
        mine[:, cols] = gathered(1, cols).astype(bf16)

    loop(width // WIDE, sum_mirror)
    back_home = remote(mine, theirs, ps_sem.at[0], pr_sem.at[0], there)
    back_home.start()

    strips(got_h, dboth, width // TILE, grad_gu, 0)

    for e in range(2):
        landed(back_f.at[e, pl.ds(CAP, HALF - CAP)], ds_sem.at[e], dr_sem.at[e]).wait_recv()
    for e in range(2):
        for a in range(2):
            rows = pl.ds(a * PIECE, PIECE)
            gates = slot_gates(tab_f, e * 16 + a * 8, pick_f, e * HALF + a * PIECE)
            out_f_rows = back_f[e, rows, :].astype(f32) * gates
            back_f[e, rows, :] = out_f_rows.astype(bf16)

    def sum_fwd(t):
        cols = pl.ds(pl.multiple_of(t * WIDE, WIDE), WIDE)
        total = None
        for e in range(2):
            for a in range(2):
                pick = pick_f[pl.ds(e * HALF + a * PIECE, PIECE), :].T
                part = dot(pick, back_f[e, pl.ds(a * PIECE, PIECE), cols])
                total = part if total is None else total + part
        y_out[:, cols] = total.astype(bf16)

    loop(width // WIDE, sum_fwd)

    returned(0).wait_recv()
    back_home.wait_recv()

    def finish(dx_sum):
        def own_cols(t):
            cols = pl.ds(pl.multiple_of(t * WIDE, WIDE), WIDE)
            dx_sum[:, cols] = gathered(0, cols) + theirs[:, cols].astype(f32)

        loop(width // WIDE, own_cols)

        def some(i):
            rows = pl.ds(pl.multiple_of(i * 32, 32), 32)
            v = x_b[rows, :].astype(f32)
            scale = lax.rsqrt(jnp.mean(v * v, axis=-1, keepdims=True) + norm_eps)
            hat = v * scale
            q = gain[...] * dx_sum[rows, :]
            dx = scale * (q - hat * jnp.mean(hat * q, axis=-1, keepdims=True))
            dx_out[rows, :] = dx.astype(bf16)

        loop(x_b.shape[0] // 32, some)

    pl.run_scoped(finish, pltpu.VMEM((128, width), f32))

    for copy in over:
        copy.wait_send()
    back_home.wait_send()
    for a in range(2):
        for e in range(2):
            landed(got_f.at[e, span(0, a)], fs_sem.at[a, e], fr_sem.at[a, e]).wait_send()
        for r in range(2):
            where = span(r * HALF, a)
            landed(got_h.at[where], hs_sem.at[r, a], hr_sem.at[r, a]).wait_send()
            landed(got_c.at[where], cs_sem.at[r, a], cr_sem.at[r, a]).wait_send()
    for e in range(2):
        landed(back_f.at[e, pl.ds(CAP, HALF - CAP)], ds_sem.at[e], dr_sem.at[e]).wait_send()
    for r in range(2):
        returned(r).wait_send()


def slot_table(routes, gates, experts):
    names = routes[:, :, None] == experts[None, None, :]
    chosen = jnp.any(names, axis=1)
    gate = jnp.sum(jnp.where(names, gates[:, :, None], 0.0), axis=1)
    tokens = routes.shape[0]
    earlier = jnp.tri(tokens, tokens, -1, dtype=bf16)
    slot = jnp.where(chosen, dot(earlier, chosen.astype(bf16)), -1.0)
    return jnp.stack([slot.T, gate.T])


def per_device(
    x_fwd, gate_fwd, route_fwd, x_bwd, gate_bwd, route_bwd, cotangent, norm_gain, w_gate_up, w_down
):
    tokens, width = x_fwd.shape
    units = w_down.shape[2]

    _, half, z, xl, c = place()
    k = jnp.arange(32, dtype=jnp.int32)
    s, second = k % 16, k // 16

    def device_of(flip):
        return ((z + s % 4) % 4) * 4 + ((xl + flip + s // 8) % 2) * 2 + (c + (s // 4) % 2) % 2

    table_f = slot_table(route_fwd, gate_fwd, 2 * device_of(0) + second)
    table_b = slot_table(route_bwd, gate_bwd, 2 * device_of(second) + (half + second) % 2)

    rows = 32 * CAP
    anywhere = pl.BlockSpec(memory_space=pl.ANY)
    vmem = pl.BlockSpec(memory_space=pltpu.VMEM)
    dma = pltpu.SemaphoreType.DMA

    def hold(*shape, dtype=bf16):
        return pltpu.VMEM(shape, dtype)

    y_fwd, dx_bwd, grad_gu, grad_dn = pl.pallas_call(
        kernel,
        out_shape=(
            jax.ShapeDtypeStruct((tokens, width), bf16),
            jax.ShapeDtypeStruct((tokens, width), bf16),
            jax.ShapeDtypeStruct((width, width), bf16),
            jax.ShapeDtypeStruct((units, width), bf16),
        ),
        in_specs=[vmem] * 7 + [anywhere] * 2,
        out_specs=(vmem, vmem, anywhere, anywhere),
        scratch_shapes=[
            hold(tokens, width),
            hold(tokens, width),
            hold(2, 16, tokens, dtype=f32),
            hold(tokens, width),
            hold(tokens, width),
            hold(rows, tokens),
            hold(rows, tokens),
            hold(2, HALF, width),
            hold(rows, width),
            hold(rows, width),
            hold(2, HALF, width),
            hold(rows, width),
            hold(rows, width),
            hold(2, width, width),
            hold(2, units, width),
            hold(2, HALF, width),
            hold(rows, width),
            hold(2, HALF, width),
            hold(rows, width),
            hold(PIECE, units),
            hold(rows, units),
            hold(rows, width),
            hold(TILE, rows),
            hold(2, TILE, width),
            hold(tokens, width),
            hold(tokens, width),
            dma((2,)), dma((6,)), dma((3,)), dma((3,)), dma((2, 2)), dma((2, 2)),
            dma((2, 2)), dma((2, 2)), dma((2, 2)), dma((2, 2)),
            dma((2,)), dma((2,)), dma((2,)), dma((2,)), dma((1,)), dma((1,)), dma((2,)),
        ],
        compiler_params=pltpu.CompilerParams(
            collective_id=0, has_side_effects=True, vmem_limit_bytes=67043328
        ),
    )(
        x_fwd,
        x_bwd,
        cotangent,
        norm_gain.reshape(1, width),
        table_f,
        table_b[:, :16],
        table_b[:, 16:],
        w_gate_up[0],
        w_down[0],
    )
    return y_fwd, dx_bwd, grad_gu[None, None], grad_dn[None, None]


def solution(mesh):
    rows = P(("pipe", "expert"), None)
    weights = P("pipe", "expert", None, None)
    return jax.shard_map(
        per_device,
        mesh=mesh,
        in_specs=(rows,) * 7 + (P(), weights, weights),
        out_specs=(rows, rows, weights, weights),
        check_vma=False,
    )
```

```python
import jax
import jax.numpy as jnp
from jax import lax
from jax.experimental import pallas as pl
from jax.experimental.pallas import tpu as pltpu
from jax.sharding import PartitionSpec as P

norm_eps = 1e-06
bf16 = jnp.bfloat16
f32 = jnp.float32
MESH = pl.DeviceIdType.MESH
CAP = 32
TILE = 256
WIDE = 512
PIECE = 8 * CAP
NT = (((1,), (1,)), ((), ()))


def place():
    p, d = lax.axis_index("pipe"), lax.axis_index("expert")
    return p, p // 4, d // 4, (d // 2) % 2, d % 2


def peer(kz, kx, kc, kh):
    p, _, z, xl, c = place()
    return p + kh * (7 - 2 * p), ((z + kz + 4) % 4) * 4 + ((xl + kx) % 2) * 2 + (c + kc) % 2


def dot(a, b):
    return jnp.dot(a, b, preferred_element_type=f32)


def dot_nt(a, b):
    return lax.dot_general(a, b, NT, preferred_element_type=f32)


def loop(count, body):
    def step(i, _):
        body(i)
        return 0

    lax.fori_loop(0, count, step, 0)


def kernel(
    x_f, x_b, cot, gain, tab_f, tab_b, w_gu, w_dn,
    y_out, dx_out, grad_gu, grad_dn,
    zx, ztab, mx, mc, mtab, normed, pick_f, pick_b, sent_f, sent_h, sent_c, got_f, got_h, got_c,
    gu, dn, out_f, out_dh, back_f, back_dh, hid_f, hid, dboth, lhs_t, gout, sums_f, sums_b, total,
    w_sem, own_sem, zs_sem, zr_sem, ms_sem, mr_sem, fs_sem, fr_sem, hs_sem, hr_sem, cs_sem, cr_sem,
    ds_sem, dr_sem, es_sem, er_sem, qs_sem, qr_sem, ps_sem, pr_sem, g_sem,
):
    width = got_h.shape[1]
    units = dn.shape[1]
    half = place()[1]
    here = peer(0, 0, 0, 0)

    def remote(src, dst, ssem, rsem, to):
        return pltpu.make_async_remote_copy(
            src_ref=src, dst_ref=dst, send_sem=ssem, recv_sem=rsem, device_id=to, device_id_type=MESH
        )

    def landed(dst, ssem, rsem):
        return remote(dst, dst, ssem, rsem, here)

    barrier = pltpu.get_barrier_semaphore()
    others = [(kz, 0, kc, 0) for kc in range(2) for kz in range(4)][1:]
    others += [(0, 1, 0, 0), (0, 1, 1, 0), (0, 0, 0, 1), (0, 1, 0, 1)]
    for other in others:
        pl.semaphore_signal(barrier, inc=1, device_id=peer(*other), device_id_type=MESH)

    weights = [
        pltpu.make_async_copy(w_gu, gu, w_sem.at[0]),
        pltpu.make_async_copy(w_dn, dn, w_sem.at[1]),
    ]
    for copy in weights:
        copy.start()

    def normalize(src, dst):
        def some(i):
            rows = pl.ds(pl.multiple_of(i * 32, 32), 32)
            v = src[rows, :].astype(f32)
            scale = lax.rsqrt(jnp.mean(v * v, axis=-1, keepdims=True) + norm_eps)
            dst[rows, :] = (v * scale * gain[...]).astype(bf16)

        loop(src.shape[0] // 32, some)

    def picks(slots, dst):
        want = lax.broadcasted_iota(jnp.int32, (8, CAP, 128), 1).astype(f32)
        hit = jnp.where(slots[:, None, :] == want, 1.0, 0.0).reshape(PIECE, 128)
        dst[...] = hit.astype(bf16)

    def slot_gates(gates, pick):
        each = jnp.broadcast_to(gates[:, None, :], (8, CAP, 128)).reshape(PIECE, 128)
        return jnp.sum(pick[...].astype(f32) * each, axis=1, keepdims=True)

    def wide(body):
        loop(width // WIDE, lambda t: body(pl.ds(pl.multiple_of(t * WIDE, WIDE), WIDE)))

    def over_z(k):
        return [
            remote(x_f, zx.at[k - 1], zs_sem.at[0, k - 1], zr_sem.at[0, k - 1], peer(k, 0, 0, 0)),
            remote(
                tab_f.at[k], ztab.at[k - 1], zs_sem.at[1, k - 1], zr_sem.at[1, k - 1],
                peer(k, 0, 0, 0),
            ),
        ]

    def over_x(r):
        to = peer(0, r % 2, 0, r // 2)
        i = r - 1
        return [
            remote(x_b, mx.at[i], ms_sem.at[0, i], mr_sem.at[0, i], to),
            remote(cot, mc.at[i], ms_sem.at[1, i], mr_sem.at[1, i], to),
            remote(tab_b.at[r], mtab.at[i], ms_sem.at[2, i], mr_sem.at[2, i], to),
        ]

    raw_z = [over_z(k) for k in (1, 2, 3)]
    raw_x = [over_x(r) for r in (1, 2, 3)]

    def send_fwd(e, slot):
        return remote(
            sent_f.at[e * 4 + slot], got_f.at[e, slot], fs_sem.at[e, slot - 1], fr_sem.at[e, slot - 1],
            peer(0, slot // 2, slot % 2, 0),
        )

    def return_fwd(e, slot):
        return remote(
            out_f.at[e, slot], back_f.at[e * 4 + slot], ds_sem.at[e, slot - 1],
            dr_sem.at[e, slot - 1], peer(0, slot // 2, slot % 2, 0),
        )

    def send_bwd(r):
        def go(j, _):
            to = peer(j % 4, 0, j // 4, 0)
            rows = pl.ds(r * PIECE + j * CAP, CAP)
            remote(sent_h.at[rows], got_h.at[rows], hs_sem.at[r], hr_sem.at[r], to).start()
            remote(sent_c.at[rows], got_c.at[rows], cs_sem.at[r], cr_sem.at[r], to).start()
            return 0

        lax.fori_loop(1, 8, go, 0)
        first = pl.ds(r * PIECE, CAP)
        pltpu.make_async_copy(sent_h.at[first], got_h.at[first], own_sem.at[0, r]).start()
        pltpu.make_async_copy(sent_c.at[first], got_c.at[first], own_sem.at[1, r]).start()

    def return_bwd(r):
        def go(j, _):
            to = peer(-(j % 4), 0, j // 4, 0)
            rows = pl.ds(r * PIECE + j * CAP, CAP)
            remote(out_dh.at[rows], back_dh.at[rows], es_sem.at[r], er_sem.at[r], to).start()
            return 0

        lax.fori_loop(1, 8, go, 0)
        first = pl.ds(r * PIECE, CAP)
        pltpu.make_async_copy(out_dh.at[first], back_dh.at[first], own_sem.at[2, r]).start()

    def rest(r):
        return pl.ds(r * PIECE + CAP, PIECE - CAP)

    def all_of(ref, r):
        return ref.at[pl.ds(r * PIECE, CAP)]

    def forward_piece(a, e):
        def first(t):
            at = pl.multiple_of(t * TILE, TILE)
            x = got_f[e, 2 * a : 2 * a + 2].reshape(PIECE, width)
            gate = dot(x, gu[e, :, pl.ds(at, TILE)])
            up = dot(x, gu[e, :, pl.ds(units + at, TILE)])
            hid_f[:, pl.ds(at, TILE)] = (gate * jax.nn.sigmoid(gate) * up).astype(bf16)

        loop(units // TILE, first)

        def second(t):
            cols = pl.ds(pl.multiple_of(t * TILE, TILE), TILE)
            rows = dot(hid_f[...], dn[e, :, cols]).astype(bf16)
            out_f[e, 2 * a : 2 * a + 2, :, :, cols] = rows.reshape(2, 4, CAP, TILE)

        loop(width // TILE, second)

    def backward_chain(r):
        rows = pl.ds(r * PIECE, PIECE)

        def first(t):
            at = pl.multiple_of(t * TILE, TILE)
            cols = pl.ds(at, TILE)
            more = pl.ds(units + at, TILE)
            x = got_h[rows, :]
            gate = dot(x, gu[half, :, cols])
            up = dot(x, gu[half, :, more])
            back = dot_nt(got_c[rows, :], dn[half, cols, :])
            squash = jax.nn.sigmoid(gate)
            active = gate * squash
            hid[rows, cols] = (active * up).astype(bf16)
            dboth[rows, cols] = (back * up * squash * (1.0 + gate * (1.0 - squash))).astype(bf16)
            dboth[rows, more] = (back * active).astype(bf16)

        loop(units // TILE, first)

        def second(t):
            cols = pl.ds(pl.multiple_of(t * TILE, TILE), TILE)
            out_dh[rows, cols] = dot_nt(dboth[rows, :], gu[half, cols, :]).astype(bf16)

        loop(width // TILE, second)

    def strips(lhs, rhs, count, dst, buf):
        def strip(m):
            at = pl.multiple_of(m * TILE, TILE)
            lhs_t[...] = lhs[:, pl.ds(at, TILE)].T

            def cols_of(t):
                cols = pl.ds(pl.multiple_of(t * TILE, TILE), TILE)
                gout[buf, :, cols] = dot(lhs_t[...], rhs[:, cols]).astype(bf16)

            loop(width // TILE, cols_of)
            copy = pltpu.make_async_copy(gout.at[buf], dst.at[pl.ds(at, TILE)], g_sem.at[buf])
            copy.start()
            copy.wait()

        loop(count, strip)

    def dispatch_fwd(b, table):
        picks(table[0], pick_f.at[b])

        def some(cols):
            rows = dot(pick_f[b], normed[:, cols]).astype(bf16)
            sent_f[:, b, :, cols] = rows.reshape(8, CAP, WIDE)

        wide(some)

    def dispatch_bwd(r, table, c_rows):
        picks(table[0], pick_b.at[r])
        gates = slot_gates(table[1], pick_b.at[r])
        rows = pl.ds(r * PIECE, PIECE)

        def some(cols):
            sent_h[rows, cols] = dot(pick_b[r], normed[:, cols]).astype(bf16)
            sent_c[rows, cols] = (dot(pick_b[r], c_rows[:, cols]) * gates).astype(bf16)

        wide(some)

    normalize(x_b, normed)
    pl.semaphore_wait(barrier, len(others))
    for copies in raw_z + [raw_x[0], raw_x[2], raw_x[1]]:
        for copy in copies:
            copy.start()
    dispatch_bwd(0, tab_b.at[0], cot)
    send_bwd(0)

    normalize(x_f, normed)
    dispatch_fwd(0, tab_f.at[0])
    for k in (1, 3, 2):
        for copy in raw_z[k - 1]:
            copy.wait_recv()
        normalize(zx.at[k - 1], normed)
        dispatch_fwd(k, ztab.at[k - 1])
    own_f = [
        pltpu.make_async_copy(sent_f.at[e * 4], got_f.at[e, 0], own_sem.at[3, e]) for e in range(2)
    ]
    for copy in own_f:
        copy.start()
    for slot in (2, 3, 1):
        for e in range(2):
            send_fwd(e, slot).start()
    for r in (1, 3, 2):
        for copy in raw_x[r - 1]:
            copy.wait_recv()
        normalize(mx.at[r - 1], normed)
        dispatch_bwd(r, mtab.at[r - 1], mc.at[r - 1])
        send_bwd(r)
    for copy in weights + own_f:
        copy.wait()

    def forward(a):
        for e in range(2):
            for slot in (2 * a, 2 * a + 1):
                if slot:
                    send_fwd(e, slot).wait_recv()
        for e in range(2):
            forward_piece(a, e)
            for slot in (2 * a, 2 * a + 1):
                if slot:
                    return_fwd(e, slot).start()

    def backward(r):
        landed(got_h.at[rest(r)], hs_sem.at[r], hr_sem.at[r]).wait_recv()
        landed(got_c.at[rest(r)], cs_sem.at[r], cr_sem.at[r]).wait_recv()
        pltpu.make_async_copy(all_of(sent_h, r), all_of(got_h, r), own_sem.at[0, r]).wait()
        pltpu.make_async_copy(all_of(sent_c, r), all_of(got_c, r), own_sem.at[1, r]).wait()
        backward_chain(r)
        return_bwd(r)

    forward(0)
    backward(0)
    backward(1)
    forward(1)
    home = [
        pltpu.make_async_copy(out_f.at[e, 0], back_f.at[e * 4], own_sem.at[3, e]) for e in range(2)
    ]
    for copy in home:
        copy.start()
    backward(3)
    backward(2)
    strips(hid, got_c, units // TILE, grad_dn, 1)

    def returned(r):
        return landed(back_dh.at[rest(r)], es_sem.at[r], er_sem.at[r])

    def gathered_bwd(r, cols):
        return dot(pick_b[r].T, back_dh[pl.ds(r * PIECE, PIECE), cols])

    def home_bwd(r):
        returned(r).wait_recv()
        pltpu.make_async_copy(all_of(out_dh, r), all_of(back_dh, r), own_sem.at[2, r]).wait()

    back_x = []
    for r in (1, 3, 2):
        home_bwd(r)

        def sum_block(cols):
            mx[r - 1, :, cols] = gathered_bwd(r, cols).astype(bf16)

        wide(sum_block)
        copy = remote(
            mx.at[r - 1], sums_b.at[r - 1], ps_sem.at[r - 1], pr_sem.at[r - 1],
            peer(0, r % 2, 0, r // 2),
        )
        copy.start()
        back_x.append(copy)

    for e in range(2):
        for slot in (1, 2, 3):
            return_fwd(e, slot).wait_recv()
    for copy in home:
        copy.wait()

    def gated_rows(b, table):
        gates = slot_gates(table[1], pick_f.at[b])
        rows = back_f[:, b].reshape(PIECE, width).astype(f32) * gates
        lhs = rows.astype(bf16)
        back_f[:, b] = lhs.reshape(8, CAP, width)

    def gathered_fwd(b, cols):
        return dot(pick_f[b].T, back_f[:, b, :, cols].reshape(PIECE, WIDE))

    back_z = []
    for b in (2, 1, 3):
        gated_rows(b, ztab.at[b - 1])

        def sum_rows(cols):
            zx[b - 1, :, cols] = gathered_fwd(b, cols).astype(bf16)

        wide(sum_rows)
        copy = remote(
            zx.at[b - 1], sums_f.at[b - 1], qs_sem.at[b - 1], qr_sem.at[b - 1], peer(-b, 0, 0, 0)
        )
        copy.start()
        back_z.append(copy)
    gated_rows(0, tab_f.at[0])

    strips(got_h, dboth, width // TILE, grad_gu, 0)

    home_bwd(0)

    def own_dh(cols):
        total[:, cols] = gathered_bwd(0, cols)

    wide(own_dh)
    for copy in back_z:
        copy.wait_recv()

    def own_y(cols):
        y = gathered_fwd(0, cols)
        for i in range(3):
            y = y + sums_f[i, :, cols].astype(f32)
        y_out[:, cols] = y.astype(bf16)

    wide(own_y)
    for copy in back_x:
        copy.wait_recv()

    def finish(i):
        rows = pl.ds(pl.multiple_of(i * 32, 32), 32)
        v = x_b[rows, :].astype(f32)
        scale = lax.rsqrt(jnp.mean(v * v, axis=-1, keepdims=True) + norm_eps)
        hat = v * scale
        dh = total[rows, :]
        for n in range(3):
            dh = dh + sums_b[n, rows, :].astype(f32)
        q = gain[...] * dh
        dx = scale * (q - hat * jnp.mean(hat * q, axis=-1, keepdims=True))
        dx_out[rows, :] = dx.astype(bf16)

    loop(x_b.shape[0] // 32, finish)

    for copies in raw_z + raw_x:
        for copy in copies:
            copy.wait_send()
    for copy in back_x + back_z:
        copy.wait_send()
    for e in range(2):
        for slot in (1, 2, 3):
            send_fwd(e, slot).wait_send()
            return_fwd(e, slot).wait_send()
    for r in range(4):
        landed(got_h.at[rest(r)], hs_sem.at[r], hr_sem.at[r]).wait_send()
        landed(got_c.at[rest(r)], cs_sem.at[r], cr_sem.at[r]).wait_send()
        returned(r).wait_send()


def slot_table(routes, gates, experts):
    names = routes[:, :, None] == experts[None, None, :]
    chosen = jnp.any(names, axis=1)
    gate = jnp.sum(jnp.where(names, gates[:, :, None], 0.0), axis=1)
    tokens = routes.shape[0]
    earlier = jnp.tri(tokens, tokens, -1, dtype=bf16)
    slot = jnp.where(chosen, dot(earlier, chosen.astype(bf16)), -1.0)
    return jnp.stack([slot.T.reshape(4, 8, tokens), gate.T.reshape(4, 8, tokens)], axis=1)


def per_device(
    x_fwd, gate_fwd, route_fwd, x_bwd, gate_bwd, route_bwd, cotangent, norm_gain, w_gate_up, w_down
):
    tokens, width = x_fwd.shape
    units = w_down.shape[2]

    _, half, z, xl, c = place()
    k = jnp.arange(32, dtype=jnp.int32)
    agent, s = k // 8, k % 8
    core = (c + s // 4) % 2
    d_f = ((z + agent) % 4) * 4 + ((xl + (s // 2) % 2) % 2) * 2 + (c + s % 2) % 2
    d_b = ((z + s % 4) % 4) * 4 + ((xl + agent % 2) % 2) * 2 + core
    table_f = slot_table(route_fwd, gate_fwd, 2 * d_f + s // 4)
    table_b = slot_table(route_bwd, gate_bwd, 2 * d_b + (half + agent // 2) % 2)

    rows = 32 * CAP
    anywhere = pl.BlockSpec(memory_space=pl.ANY)
    vmem = pl.BlockSpec(memory_space=pltpu.VMEM)
    dma = pltpu.SemaphoreType.DMA

    def hold(*shape, dtype=bf16):
        return pltpu.VMEM(shape, dtype)

    y_fwd, dx_bwd, grad_gu, grad_dn = pl.pallas_call(
        kernel,
        out_shape=(
            jax.ShapeDtypeStruct((tokens, width), bf16),
            jax.ShapeDtypeStruct((tokens, width), bf16),
            jax.ShapeDtypeStruct((width, width), bf16),
            jax.ShapeDtypeStruct((units, width), bf16),
        ),
        in_specs=[vmem] * 6 + [anywhere] * 2,
        out_specs=(vmem, vmem, anywhere, anywhere),
        scratch_shapes=[
            hold(3, tokens, width),
            hold(3, 2, 8, tokens, dtype=f32),
            hold(3, tokens, width),
            hold(3, tokens, width),
            hold(3, 2, 8, tokens, dtype=f32),
            hold(tokens, width),
            hold(4, PIECE, tokens),
            hold(4, PIECE, tokens),
            hold(8, 4, CAP, width),
            hold(rows, width),
            hold(rows, width),
            hold(2, 4, 4, CAP, width),
            hold(rows, width),
            hold(rows, width),
            hold(2, width, width),
            hold(2, units, width),
            hold(2, 4, 4, CAP, width),
            hold(rows, width),
            hold(8, 4, CAP, width),
            hold(rows, width),
            hold(PIECE, units),
            hold(rows, units),
            hold(rows, width),
            hold(TILE, rows),
            hold(2, TILE, width),
            hold(3, tokens, width),
            hold(3, tokens, width),
            hold(tokens, width, dtype=f32),
            dma((2,)), dma((4, 4)), dma((2, 3)), dma((2, 3)), dma((3, 3)), dma((3, 3)),
            dma((2, 3)), dma((2, 3)), dma((4,)), dma((4,)), dma((4,)), dma((4,)),
            dma((2, 3)), dma((2, 3)), dma((4,)), dma((4,)), dma((3,)), dma((3,)),
            dma((3,)), dma((3,)), dma((2,)),
        ],
        compiler_params=pltpu.CompilerParams(
            collective_id=0, has_side_effects=True, vmem_limit_bytes=67043328
        ),
    )(
        x_fwd,
        x_bwd,
        cotangent,
        norm_gain.reshape(1, width),
        table_f,
        table_b,
        w_gate_up[0],
        w_down[0],
    )
    return y_fwd, dx_bwd, grad_gu[None, None], grad_dn[None, None]


def solution(mesh):
    rows = P(("pipe", "expert"), None)
    weights = P("pipe", "expert", None, None)
    return jax.shard_map(
        per_device,
        mesh=mesh,
        in_specs=(rows,) * 7 + (P(), weights, weights),
        out_specs=(rows, rows, weights, weights),
        check_vma=False,
    )
```

```python
import jax
import jax.numpy as jnp
from jax import lax
from jax.experimental import pallas as pl
from jax.experimental.pallas import tpu as pltpu
from jax.sharding import PartitionSpec as P

norm_eps = 1e-06
bf16 = jnp.bfloat16
f32 = jnp.float32
MESH = pl.DeviceIdType.MESH
CAP = 32
TILE = 256
WIDE = 512
PIECE = 8 * CAP
NT = (((1,), (1,)), ((), ()))


def place():
    p, d = lax.axis_index("pipe"), lax.axis_index("expert")
    return p, p // 4, d // 4, (d // 2) % 2, d % 2


def peer(kz, kx, kc, kh):
    p, _, z, xl, c = place()
    return p + kh * (7 - 2 * p), ((z + kz + 4) % 4) * 4 + ((xl + kx) % 2) * 2 + (c + kc) % 2


def dot(a, b):
    return jnp.dot(a, b, preferred_element_type=f32)


def dot_nt(a, b):
    return lax.dot_general(a, b, NT, preferred_element_type=f32)


def loop(count, body):
    def step(i, _):
        body(i)
        return 0

    lax.fori_loop(0, count, step, 0)


def kernel(
    x_f, x_b, cot, gain, tab_f, tab_b, w_gu, w_dn,
    y_out, dx_out, grad_gu, grad_dn,
    zx, ztab, mx, mc, mtab, normed, pick_f, pick_b, pick_e, sent_f, sent_h, sent_c, got_f, got_h, got_c,
    gu, dn, out_f, out_dh, back_f, back_dh, hid_f, hid, dboth, lhs_t, gout, sums_f, sums_b, total,
    w_sem, own_sem, zs_sem, zr_sem, ms_sem, mr_sem, fs_sem, fr_sem, hs_sem, hr_sem, cs_sem, cr_sem,
    ds_sem, dr_sem, es_sem, er_sem, qs_sem, qr_sem, ps_sem, pr_sem, g_sem,
):
    width = got_h.shape[1]
    units = dn.shape[1]
    half = place()[1]
    here = peer(0, 0, 0, 0)

    def remote(src, dst, ssem, rsem, to):
        return pltpu.make_async_remote_copy(
            src_ref=src, dst_ref=dst, send_sem=ssem, recv_sem=rsem, device_id=to, device_id_type=MESH
        )

    def landed(dst, ssem, rsem):
        return remote(dst, dst, ssem, rsem, here)

    barrier = pltpu.get_barrier_semaphore()
    others = [(kz, 0, kc, 0) for kc in range(2) for kz in range(4)][1:]
    others += [(0, n % 2, (n // 2) % 2, n // 4) for n in (1, 3, 4, 5, 6, 7)]
    for other in others:
        pl.semaphore_signal(barrier, inc=1, device_id=peer(*other), device_id_type=MESH)

    weights = [
        pltpu.make_async_copy(w_gu, gu, w_sem.at[0]),
        pltpu.make_async_copy(w_dn, dn, w_sem.at[1]),
    ]
    for copy in weights:
        copy.start()

    def normalize(src, dst):
        def some(i):
            rows = pl.ds(pl.multiple_of(i * 32, 32), 32)
            v = src[rows, :].astype(f32)
            scale = lax.rsqrt(jnp.mean(v * v, axis=-1, keepdims=True) + norm_eps)
            dst[rows, :] = (v * scale * gain[...]).astype(bf16)

        loop(src.shape[0] // 32, some)

    def picks(slots, dst):
        want = lax.broadcasted_iota(jnp.int32, (8, CAP, 128), 1).astype(f32)
        hit = jnp.where(slots[:, None, :] == want, 1.0, 0.0).reshape(PIECE, 128)
        dst[...] = hit.astype(bf16)

    def slot_gates(gates, pick):
        each = jnp.broadcast_to(gates[:, None, :], (8, CAP, 128)).reshape(PIECE, 128)
        return jnp.sum(pick[...].astype(f32) * each, axis=1, keepdims=True)

    def wide(body):
        loop(width // WIDE, lambda t: body(pl.ds(pl.multiple_of(t * WIDE, WIDE), WIDE)))

    def over_z(k):
        return [
            remote(x_f, zx.at[k - 1], zs_sem.at[0, k - 1], zr_sem.at[0, k - 1], peer(k, 0, 0, 0)),
            remote(
                tab_f.at[k], ztab.at[k - 1], zs_sem.at[1, k - 1], zr_sem.at[1, k - 1],
                peer(k, 0, 0, 0),
            ),
        ]

    def over_x(r):
        to = peer(0, r % 2, 0, r // 2)
        by = peer(0, 1, 0, 1) if r == 2 else to
        i = r - 1
        rows, cots = (mx.at[0], mc.at[0]) if r == 2 else (x_b, cot)
        return [
            remote(tab_b.at[r], mtab.at[i], ms_sem.at[2, i], mr_sem.at[2, i], to),
            remote(rows, mx.at[i], ms_sem.at[0, i], mr_sem.at[0, i], by),
            remote(cots, mc.at[i], ms_sem.at[1, i], mr_sem.at[1, i], by),
        ]

    raw_z = [over_z(k) for k in (1, 2, 3)]
    raw_x = [over_x(r) for r in (1, 2, 3)]

    def send_fwd(e, slot):
        return remote(
            sent_f.at[e * 4 + slot], got_f.at[e, slot], fs_sem.at[e, slot - 1], fr_sem.at[e, slot - 1],
            peer(0, slot // 2, slot % 2, 0),
        )

    def return_fwd(e, slot):
        return remote(
            out_f.at[e, slot], back_f.at[e * 4 + slot], ds_sem.at[e, slot - 1],
            dr_sem.at[e, slot - 1], peer(0, slot // 2, slot % 2, 0),
        )

    def send_bwd(r):
        def go(j, _):
            to = peer(j % 4, 0, j // 4, 0)
            rows = pl.ds(r * PIECE + j * CAP, CAP)
            remote(sent_h.at[rows], got_h.at[rows], hs_sem.at[r], hr_sem.at[r], to).start()
            remote(sent_c.at[rows], got_c.at[rows], cs_sem.at[r], cr_sem.at[r], to).start()
            return 0

        lax.fori_loop(1, 8, go, 0)
        first = pl.ds(r * PIECE, CAP)
        pltpu.make_async_copy(sent_h.at[first], got_h.at[first], own_sem.at[0, r]).start()
        pltpu.make_async_copy(sent_c.at[first], got_c.at[first], own_sem.at[1, r]).start()

    def return_bwd(r, kc):
        i = r * 2 + kc
        return remote(
            out_dh.at[i], back_dh.at[i], es_sem.at[i - 1], er_sem.at[i - 1],
            peer(0, r % 2, kc, r // 2),
        )

    def rest(r):
        return pl.ds(r * PIECE + CAP, PIECE - CAP)

    def all_of(ref, r):
        return ref.at[pl.ds(r * PIECE, CAP)]

    def forward_piece(a, e):
        def first(t):
            at = pl.multiple_of(t * TILE, TILE)
            x = got_f[e, 2 * a : 2 * a + 2].reshape(PIECE, width)
            gate = dot(x, gu[e, :, pl.ds(at, TILE)])
            up = dot(x, gu[e, :, pl.ds(units + at, TILE)])
            hid_f[:, pl.ds(at, TILE)] = (gate * jax.nn.sigmoid(gate) * up).astype(bf16)

        loop(units // TILE, first)

        def second(t):
            cols = pl.ds(pl.multiple_of(t * TILE, TILE), TILE)
            rows = dot(hid_f[...], dn[e, :, cols]).astype(bf16)
            out_f[e, 2 * a : 2 * a + 2, :, :, cols] = rows.reshape(2, 4, CAP, TILE)

        loop(width // TILE, second)

    def backward_chain(r):
        rows = pl.ds(r * PIECE, PIECE)

        def first(t):
            at = pl.multiple_of(t * TILE, TILE)
            cols = pl.ds(at, TILE)
            more = pl.ds(units + at, TILE)
            x = got_h[rows, :]
            gate = dot(x, gu[half, :, cols])
            up = dot(x, gu[half, :, more])
            back = dot_nt(got_c[rows, :], dn[half, cols, :])
            squash = jax.nn.sigmoid(gate)
            active = gate * squash
            hid[rows, cols] = (active * up).astype(bf16)
            dboth[rows, cols] = (back * up * squash * (1.0 + gate * (1.0 - squash))).astype(bf16)
            dboth[rows, more] = (back * active).astype(bf16)

        loop(units // TILE, first)

        def second(t):
            cols = pl.ds(pl.multiple_of(t * TILE, TILE), TILE)
            dh = dot_nt(dboth[rows, :], gu[half, cols, :]).astype(bf16)
            out_dh[2 * r : 2 * r + 2, :, :, cols] = dh.reshape(2, 4, CAP, TILE)

        loop(width // TILE, second)

    def strips(lhs, rhs, count, dst, buf):
        def strip(m):
            at = pl.multiple_of(m * TILE, TILE)
            lhs_t[...] = lhs[:, pl.ds(at, TILE)].T

            def cols_of(t):
                cols = pl.ds(pl.multiple_of(t * TILE, TILE), TILE)
                gout[buf, :, cols] = dot(lhs_t[...], rhs[:, cols]).astype(bf16)

            loop(width // TILE, cols_of)
            copy = pltpu.make_async_copy(gout.at[buf], dst.at[pl.ds(at, TILE)], g_sem.at[buf])
            copy.start()
            copy.wait()

        loop(count, strip)

    def dispatch_fwd(b, table):
        picks(table[0], pick_f.at[b])

        def some(cols):
            rows = dot(pick_f[b], normed[:, cols]).astype(bf16)
            sent_f[:, b, :, cols] = rows.reshape(8, CAP, WIDE)

        wide(some)

    def dispatch_bwd(r, table, c_rows):
        picks(table[0], pick_b.at[r])
        gates = slot_gates(table[1], pick_b.at[r])
        rows = pl.ds(r * PIECE, PIECE)

        def some(cols):
            sent_h[rows, cols] = dot(pick_b[r], normed[:, cols]).astype(bf16)
            sent_c[rows, cols] = (dot(pick_b[r], c_rows[:, cols]) * gates).astype(bf16)

        wide(some)

    normalize(x_b, normed)
    pl.semaphore_wait(barrier, len(others))
    for copies in (raw_z[0], raw_z[2], raw_z[1], raw_x[0], raw_x[2], raw_x[1][:1]):
        for copy in copies:
            copy.start()
    dispatch_bwd(0, tab_b.at[0], cot)

    normalize(x_f, normed)
    dispatch_fwd(0, tab_f.at[0])
    for k in (1, 3, 2):
        for copy in raw_z[k - 1]:
            copy.wait_recv()
        normalize(zx.at[k - 1], normed)
        dispatch_fwd(k, ztab.at[k - 1])
    own_f = [
        pltpu.make_async_copy(sent_f.at[e * 4], got_f.at[e, 0], own_sem.at[3, e]) for e in range(2)
    ]
    for copy in own_f:
        copy.start()
    for e in range(2):
        for slot in (2, 3, 1):
            send_fwd(e, slot).start()
    for r in (1, 3):
        for copy in raw_x[r - 1]:
            copy.wait_recv()
        if r == 1:
            for copy in raw_x[1][1:]:
                copy.start()
        normalize(mx.at[r - 1], normed)
        dispatch_bwd(r, mtab.at[r - 1], mc.at[r - 1])
        send_bwd(r)
    for copy in weights + own_f:
        copy.wait()

    def forward(a, e):
        for slot in (2 * a, 2 * a + 1):
            if slot:
                send_fwd(e, slot).wait_recv()
        forward_piece(a, e)
        for slot in (2 * a, 2 * a + 1):
            if slot:
                return_fwd(e, slot).start()

    def backward(r):
        landed(got_h.at[rest(r)], hs_sem.at[r], hr_sem.at[r]).wait_recv()
        landed(got_c.at[rest(r)], cs_sem.at[r], cr_sem.at[r]).wait_recv()
        pltpu.make_async_copy(all_of(sent_h, r), all_of(got_h, r), own_sem.at[0, r]).wait()
        pltpu.make_async_copy(all_of(sent_c, r), all_of(got_c, r), own_sem.at[1, r]).wait()
        backward_chain(r)
        for kc in range(2):
            if r or kc:
                return_bwd(r, kc).start()

    forward(0, 0)
    for copy in raw_x[1]:
        copy.wait_recv()
    normalize(mx.at[1], normed)
    dispatch_bwd(2, mtab.at[1], mc.at[1])
    send_bwd(2)
    send_bwd(0)
    forward(0, 1)
    forward(1, 0)
    backward(1)
    forward(1, 1)
    backward(3)
    backward(2)
    for b in range(4):
        picks((tab_f.at[0] if b == 0 else ztab.at[b - 1])[2], pick_e.at[b])
    backward(0)
    home = [
        pltpu.make_async_copy(out_f.at[e, 0], back_f.at[e * 4], own_sem.at[3, e]) for e in range(2)
    ]
    home.append(pltpu.make_async_copy(out_dh.at[0], back_dh.at[0], own_sem.at[2, 0]))
    for copy in home:
        copy.start()

    def gated_rows(b, table):
        gates = slot_gates(table[1], pick_f.at[b])
        rows = back_f[:, b].reshape(PIECE, width).astype(f32) * gates
        lhs = rows.astype(bf16)
        back_f[:, b] = lhs.reshape(8, CAP, width)

    def gathered_fwd(b, cols):
        return dot(pick_f[b].T, back_f[:, b, :, cols].reshape(PIECE, WIDE))

    def gathered_bwd(b, cols):
        return dot(pick_e[b].T, back_dh[:, b, :, cols].reshape(PIECE, WIDE))

    for e in range(2):
        for slot in (1, 2, 3):
            return_fwd(e, slot).wait_recv()
    for copy in home:
        copy.wait()
    back_z = []
    for b in (2, 1, 3):
        gated_rows(b, ztab.at[b - 1])

        def sum_rows(cols):
            zx[b - 1, :, cols] = gathered_fwd(b, cols).astype(bf16)

        wide(sum_rows)
        copy = remote(
            zx.at[b - 1], sums_f.at[b - 1], qs_sem.at[b - 1], qr_sem.at[b - 1], peer(-b, 0, 0, 0)
        )
        copy.start()
        back_z.append(copy)

    for copy in raw_x[1][1:]:
        copy.wait_send()
    for i in range(1, 8):
        return_bwd(i // 2, i % 2).wait_recv()
    back_x = []
    for b in (2, 1, 3):

        def sum_block(cols):
            mx[b - 1, :, cols] = gathered_bwd(b, cols).astype(bf16)

        wide(sum_block)
        copy = remote(
            mx.at[b - 1], sums_b.at[b - 1], ps_sem.at[b - 1], pr_sem.at[b - 1], peer(-b, 0, 0, 0)
        )
        copy.start()
        back_x.append(copy)

    def own_dh(cols):
        total[:, cols] = gathered_bwd(0, cols)

    wide(own_dh)
    gated_rows(0, tab_f.at[0])
    strips(hid, got_c, units // TILE, grad_dn, 1)
    strips(got_h, dboth, width // TILE, grad_gu, 0)

    for copy in back_z:
        copy.wait_recv()

    def own_y(cols):
        y = gathered_fwd(0, cols)
        for i in range(3):
            y = y + sums_f[i, :, cols].astype(f32)
        y_out[:, cols] = y.astype(bf16)

    wide(own_y)
    for copy in back_x:
        copy.wait_recv()

    def finish(i):
        rows = pl.ds(pl.multiple_of(i * 32, 32), 32)
        v = x_b[rows, :].astype(f32)
        scale = lax.rsqrt(jnp.mean(v * v, axis=-1, keepdims=True) + norm_eps)
        hat = v * scale
        dh = total[rows, :]
        for n in range(3):
            dh = dh + sums_b[n, rows, :].astype(f32)
        q = gain[...] * dh
        dx = scale * (q - hat * jnp.mean(hat * q, axis=-1, keepdims=True))
        dx_out[rows, :] = dx.astype(bf16)

    loop(x_b.shape[0] // 32, finish)

    for copies in raw_z + [raw_x[0], raw_x[2], raw_x[1][:1]]:
        for copy in copies:
            copy.wait_send()
    for copy in back_x + back_z:
        copy.wait_send()
    for e in range(2):
        for slot in (1, 2, 3):
            send_fwd(e, slot).wait_send()
            return_fwd(e, slot).wait_send()
    for r in range(4):
        landed(got_h.at[rest(r)], hs_sem.at[r], hr_sem.at[r]).wait_send()
        landed(got_c.at[rest(r)], cs_sem.at[r], cr_sem.at[r]).wait_send()
    for i in range(1, 8):
        return_bwd(i // 2, i % 2).wait_send()


def slot_table(routes, gates, experts):
    names = routes[:, :, None] == experts[None, None, :]
    chosen = jnp.any(names, axis=1)
    gate = jnp.sum(jnp.where(names, gates[:, :, None], 0.0), axis=1)
    tokens = routes.shape[0]
    earlier = jnp.tri(tokens, tokens, -1, dtype=bf16)
    slot = jnp.where(chosen, dot(earlier, chosen.astype(bf16)), -1.0)
    return jnp.stack([slot.T.reshape(4, 8, tokens), gate.T.reshape(4, 8, tokens)], axis=1)


def per_device(
    x_fwd, gate_fwd, route_fwd, x_bwd, gate_bwd, route_bwd, cotangent, norm_gain, w_gate_up, w_down
):
    tokens, width = x_fwd.shape
    units = w_down.shape[2]

    _, half, z, xl, c = place()
    k = jnp.arange(32, dtype=jnp.int32)
    agent, s = k // 8, k % 8
    core = (c + s // 4) % 2
    d_f = ((z + agent) % 4) * 4 + ((xl + (s // 2) % 2) % 2) * 2 + (c + s % 2) % 2
    d_b = ((z + s % 4) % 4) * 4 + ((xl + agent % 2) % 2) * 2 + core
    table_f = slot_table(route_fwd, gate_fwd, 2 * d_f + s // 4)
    table_b = slot_table(route_bwd, gate_bwd, 2 * d_b + (half + agent // 2) % 2)

    by_z = table_b[:, 0].reshape(4, 2, 4, tokens).transpose(2, 0, 1, 3).reshape(4, 1, 8, tokens)
    table_f = jnp.concatenate([table_f, by_z], axis=1)

    rows = 32 * CAP
    anywhere = pl.BlockSpec(memory_space=pl.ANY)
    vmem = pl.BlockSpec(memory_space=pltpu.VMEM)
    dma = pltpu.SemaphoreType.DMA

    def hold(*shape, dtype=bf16):
        return pltpu.VMEM(shape, dtype)

    y_fwd, dx_bwd, grad_gu, grad_dn = pl.pallas_call(
        kernel,
        out_shape=(
            jax.ShapeDtypeStruct((tokens, width), bf16),
            jax.ShapeDtypeStruct((tokens, width), bf16),
            jax.ShapeDtypeStruct((width, width), bf16),
            jax.ShapeDtypeStruct((units, width), bf16),
        ),
        in_specs=[vmem] * 6 + [anywhere] * 2,
        out_specs=(vmem, vmem, anywhere, anywhere),
        scratch_shapes=[
            hold(3, tokens, width),
            hold(3, 3, 8, tokens, dtype=f32),
            hold(3, tokens, width),
            hold(3, tokens, width),
            hold(3, 2, 8, tokens, dtype=f32),
            hold(tokens, width),
            hold(4, PIECE, tokens),
            hold(4, PIECE, tokens),
            hold(4, PIECE, tokens),
            hold(8, 4, CAP, width),
            hold(rows, width),
            hold(rows, width),
            hold(2, 4, 4, CAP, width),
            hold(rows, width),
            hold(rows, width),
            hold(2, width, width),
            hold(2, units, width),
            hold(2, 4, 4, CAP, width),
            hold(8, 4, CAP, width),
            hold(8, 4, CAP, width),
            hold(8, 4, CAP, width),
            hold(PIECE, units),
            hold(rows, units),
            hold(rows, width),
            hold(TILE, rows),
            hold(2, TILE, width),
            hold(3, tokens, width),
            hold(3, tokens, width),
            hold(tokens, width, dtype=f32),
            dma((2,)), dma((4, 4)), dma((2, 3)), dma((2, 3)), dma((3, 3)), dma((3, 3)),
            dma((2, 3)), dma((2, 3)), dma((4,)), dma((4,)), dma((4,)), dma((4,)),
            dma((2, 3)), dma((2, 3)), dma((7,)), dma((7,)), dma((3,)), dma((3,)),
            dma((3,)), dma((3,)), dma((2,)),
        ],
        compiler_params=pltpu.CompilerParams(
            collective_id=0, has_side_effects=True, vmem_limit_bytes=67043328
        ),
    )(
        x_fwd,
        x_bwd,
        cotangent,
        norm_gain.reshape(1, width),
        table_f,
        table_b,
        w_gate_up[0],
        w_down[0],
    )
    return y_fwd, dx_bwd, grad_gu[None, None], grad_dn[None, None]


def solution(mesh):
    rows = P(("pipe", "expert"), None)
    weights = P("pipe", "expert", None, None)
    return jax.shard_map(
        per_device,
        mesh=mesh,
        in_specs=(rows,) * 7 + (P(), weights, weights),
        out_specs=(rows, rows, weights, weights),
        check_vma=False,
    )
```

```python
import jax
import jax.numpy as jnp
from jax import lax
from jax.experimental import pallas as pl
from jax.experimental.pallas import tpu as pltpu
from jax.sharding import PartitionSpec as P

norm_eps = 1e-06
bf16 = jnp.bfloat16
f32 = jnp.float32
MESH = pl.DeviceIdType.MESH
CAP = 32
TILE = 256
WIDE = 512
PIECE = 8 * CAP
NT = (((1,), (1,)), ((), ()))


def place():
    p, d = lax.axis_index("pipe"), lax.axis_index("expert")
    return p, p // 4, d // 4, (d // 2) % 2, d % 2


def peer(kz, kx, kc, kh):
    p, _, z, xl, c = place()
    return p + kh * (7 - 2 * p), ((z + kz + 4) % 4) * 4 + ((xl + kx) % 2) * 2 + (c + kc) % 2


def dot(a, b):
    return jnp.dot(a, b, preferred_element_type=f32)


def dot_nt(a, b):
    return lax.dot_general(a, b, NT, preferred_element_type=f32)


def loop(count, body):
    def step(i, _):
        body(i)
        return 0

    lax.fori_loop(0, count, step, 0)


def kernel(
    x_f, x_b, cot, gain, routes_f, gates_f, routes_b, gates_b, w_gu, w_dn,
    y_out, dx_out, grad_gu, grad_dn,
    tab_f, tab_b, zx, ztab, mx, mc, mtab, normed, pick_f, pick_b, sent_f, sent_h, sent_c, got_f, got_h, got_c,
    gu, dn, out_f, out_dh, back_f, back_dh, hid_f, hid, dboth, lhs_t, gout, sums_f, sums_b, total,
    w_sem, own_sem, rs_sem, rr_sem, zs_sem, zr_sem, ms_sem, mr_sem, fs_sem, fr_sem, hs_sem, hr_sem, cs_sem, cr_sem,
    ds_sem, dr_sem, es_sem, er_sem, qs_sem, qr_sem, ps_sem, pr_sem, g_sem,
):
    width = got_h.shape[1]
    units = dn.shape[1]
    half = place()[1]
    here = peer(0, 0, 0, 0)

    def remote(src, dst, ssem, rsem, to):
        return pltpu.make_async_remote_copy(
            src_ref=src, dst_ref=dst, send_sem=ssem, recv_sem=rsem, device_id=to, device_id_type=MESH
        )

    def landed(dst, ssem, rsem):
        return remote(dst, dst, ssem, rsem, here)

    barrier = pltpu.get_barrier_semaphore()
    others = [(kz, 0, kc, 0) for kc in range(2) for kz in range(4)][1:]
    others += [(0, 1, 0, 0), (0, 1, 1, 0), (0, 0, 0, 1), (0, 1, 0, 1)]
    for other in others:
        pl.semaphore_signal(barrier, inc=1, device_id=peer(*other), device_id_type=MESH)

    weights = [
        pltpu.make_async_copy(w_gu, gu, w_sem.at[0]),
        pltpu.make_async_copy(w_dn, dn, w_sem.at[1]),
    ]
    for copy in weights:
        copy.start()

    def normalize(src, dst):
        def some(i):
            rows = pl.ds(pl.multiple_of(i * 32, 32), 32)
            v = src[rows, :].astype(f32)
            scale = lax.rsqrt(jnp.mean(v * v, axis=-1, keepdims=True) + norm_eps)
            dst[rows, :] = (v * scale * gain[...][None, :]).astype(bf16)

        loop(src.shape[0] // 32, some)

    def tables(routes, gates, experts, dst):
        chosen = jnp.zeros((32, 128), f32)
        weight = jnp.zeros((32, 128), f32)
        for n in range(routes.shape[0]):
            hit = routes[n : n + 1, :] == experts
            chosen = jnp.where(hit, 1.0, chosen)
            weight = jnp.where(hit, gates[n : n + 1, :], weight)
        row = lax.broadcasted_iota(jnp.int32, (128, 128), 0)
        col = lax.broadcasted_iota(jnp.int32, (128, 128), 1)
        earlier = jnp.where(row < col, 1.0, 0.0).astype(bf16)
        slots = jnp.where(chosen > 0.0, dot(chosen.astype(bf16), earlier), -1.0)
        dst[:, 0] = slots.reshape(4, 8, 128)
        dst[:, 1] = weight.reshape(4, 8, 128)

    def picks(slots, dst):
        want = lax.broadcasted_iota(jnp.int32, (8, CAP, 128), 1).astype(f32)
        hit = jnp.where(slots[:, None, :] == want, 1.0, 0.0).reshape(PIECE, 128)
        dst[...] = hit.astype(bf16)

    def slot_gates(gates, pick):
        each = jnp.broadcast_to(gates[:, None, :], (8, CAP, 128)).reshape(PIECE, 128)
        return jnp.sum(pick[...].astype(f32) * each, axis=1, keepdims=True)

    def wide(body):
        loop(width // WIDE, lambda t: body(pl.ds(pl.multiple_of(t * WIDE, WIDE), WIDE)))

    def over_z(k):
        table = remote(
            tab_f.at[k], ztab.at[k - 1], zs_sem.at[1, k - 1], zr_sem.at[1, k - 1], peer(k, 0, 0, 0)
        )
        if k == 2:
            return [table]
        rows = remote(
            x_f, zx.at[k - 1], zs_sem.at[0, k - 1], zr_sem.at[0, k - 1], peer(k, 0, 0, 0)
        )
        return [table, rows]

    def relay(k):
        part = pl.ds(0 if k == 1 else 64, 64)
        i = k // 2
        return remote(
            zx.at[k - 1, part], zx.at[1, part], rs_sem.at[i], rr_sem.at[i], peer(k, 0, 0, 0)
        )

    def over_x(r):
        to = peer(0, r % 2, 0, r // 2)
        i = r - 1
        return [
            remote(x_b, mx.at[i], ms_sem.at[0, i], mr_sem.at[0, i], to),
            remote(cot, mc.at[i], ms_sem.at[1, i], mr_sem.at[1, i], to),
            remote(tab_b.at[r], mtab.at[i], ms_sem.at[2, i], mr_sem.at[2, i], to),
        ]

    raw_z = [over_z(k) for k in (1, 2, 3)]
    raw_x = [over_x(r) for r in (1, 2, 3)]
    relays = [relay(1), relay(3)]

    def send_fwd(e, slot):
        return remote(
            sent_f.at[e * 4 + slot], got_f.at[e, slot], fs_sem.at[e, slot - 1], fr_sem.at[e, slot - 1],
            peer(0, slot // 2, slot % 2, 0),
        )

    def return_fwd(e, slot):
        return remote(
            out_f.at[e, slot], back_f.at[e * 4 + slot], ds_sem.at[e, slot - 1],
            dr_sem.at[e, slot - 1], peer(0, slot // 2, slot % 2, 0),
        )

    def send_bwd(r):
        def go(j, _):
            to = peer(j % 4, 0, j // 4, 0)
            rows = pl.ds(r * PIECE + j * CAP, CAP)
            remote(sent_h.at[rows], got_h.at[rows], hs_sem.at[r], hr_sem.at[r], to).start()
            remote(sent_c.at[rows], got_c.at[rows], cs_sem.at[r], cr_sem.at[r], to).start()
            return 0

        lax.fori_loop(1, 8, go, 0)
        first = pl.ds(r * PIECE, CAP)
        pltpu.make_async_copy(sent_h.at[first], got_h.at[first], own_sem.at[0, r]).start()
        pltpu.make_async_copy(sent_c.at[first], got_c.at[first], own_sem.at[1, r]).start()

    def return_bwd(r):
        def go(j, _):
            to = peer(-(j % 4), 0, j // 4, 0)
            rows = pl.ds(r * PIECE + j * CAP, CAP)
            remote(out_dh.at[rows], back_dh.at[rows], es_sem.at[r], er_sem.at[r], to).start()
            return 0

        lax.fori_loop(1, 8, go, 0)
        first = pl.ds(r * PIECE, CAP)
        pltpu.make_async_copy(out_dh.at[first], back_dh.at[first], own_sem.at[2, r]).start()

    def rest(r):
        return pl.ds(r * PIECE + CAP, PIECE - CAP)

    def all_of(ref, r):
        return ref.at[pl.ds(r * PIECE, CAP)]

    def forward_piece(a, e):
        def first(t):
            at = pl.multiple_of(t * TILE, TILE)
            x = got_f[e, 2 * a : 2 * a + 2].reshape(PIECE, width)
            gate = dot(x, gu[e, :, pl.ds(at, TILE)])
            up = dot(x, gu[e, :, pl.ds(units + at, TILE)])
            hid_f[:, pl.ds(at, TILE)] = (gate * jax.nn.sigmoid(gate) * up).astype(bf16)

        loop(units // TILE, first)

        def second(t):
            cols = pl.ds(pl.multiple_of(t * TILE, TILE), TILE)
            rows = dot(hid_f[...], dn[e, :, cols]).astype(bf16)
            out_f[e, 2 * a : 2 * a + 2, :, :, cols] = rows.reshape(2, 4, CAP, TILE)

        loop(width // TILE, second)

    def backward_chain(r):
        rows = pl.ds(r * PIECE, PIECE)

        def first(t):
            at = pl.multiple_of(t * TILE, TILE)
            cols = pl.ds(at, TILE)
            more = pl.ds(units + at, TILE)
            x = got_h[rows, :]
            gate = dot(x, gu[half, :, cols])
            up = dot(x, gu[half, :, more])
            back = dot_nt(got_c[rows, :], dn[half, cols, :])
            squash = jax.nn.sigmoid(gate)
            active = gate * squash
            hid[rows, cols] = (active * up).astype(bf16)
            dboth[rows, cols] = (back * up * squash * (1.0 + gate * (1.0 - squash))).astype(bf16)
            dboth[rows, more] = (back * active).astype(bf16)

        loop(units // TILE, first)

        def second(t):
            cols = pl.ds(pl.multiple_of(t * TILE, TILE), TILE)
            out_dh[rows, cols] = dot_nt(dboth[rows, :], gu[half, cols, :]).astype(bf16)

        loop(width // TILE, second)

    def strips(lhs, rhs, count, dst, buf):
        def strip(m):
            at = pl.multiple_of(m * TILE, TILE)
            lhs_t[...] = lhs[:, pl.ds(at, TILE)].T

            def cols_of(t):
                cols = pl.ds(pl.multiple_of(t * TILE, TILE), TILE)
                gout[buf, :, cols] = dot(lhs_t[...], rhs[:, cols]).astype(bf16)

            loop(width // TILE, cols_of)
            copy = pltpu.make_async_copy(gout.at[buf], dst.at[pl.ds(at, TILE)], g_sem.at[buf])
            copy.start()
            copy.wait()

        loop(count, strip)

    def dispatch_fwd(b, table):
        picks(table[0], pick_f.at[b])

        def some(cols):
            rows = dot(pick_f[b], normed[:, cols]).astype(bf16)
            sent_f[:, b, :, cols] = rows.reshape(8, CAP, WIDE)

        wide(some)

    def dispatch_bwd(r, table, c_rows):
        picks(table[0], pick_b.at[r])
        gates = slot_gates(table[1], pick_b.at[r])
        rows = pl.ds(r * PIECE, PIECE)

        def some(cols):
            sent_h[rows, cols] = dot(pick_b[r], normed[:, cols]).astype(bf16)
            sent_c[rows, cols] = (dot(pick_b[r], c_rows[:, cols]) * gates).astype(bf16)

        wide(some)

    _, _, z, xl, c = place()
    k = lax.broadcasted_iota(jnp.int32, (32, 128), 0)
    agent, s = k >> 3, k & 7
    d_f = ((z + agent) & 3) * 4 + ((xl + (s >> 1)) & 1) * 2 + ((c + s) & 1)
    d_b = ((z + s) & 3) * 4 + ((xl + agent) & 1) * 2 + ((c + (s >> 2)) & 1)
    tables(routes_f, gates_f, 2 * d_f + (s >> 2), tab_f)
    tables(routes_b, gates_b, 2 * d_b + ((half + (agent >> 1)) & 1), tab_b)
    normalize(x_b, normed)
    pl.semaphore_wait(barrier, len(others))
    for copies in raw_z + [raw_x[0], raw_x[2], raw_x[1]]:
        for copy in copies:
            copy.start()
    dispatch_bwd(0, tab_b.at[0], cot)

    normalize(x_f, normed)
    dispatch_fwd(0, tab_f.at[0])
    for k, copy in zip((1, 3), relays):
        for raw in raw_z[k - 1]:
            raw.wait_recv()
        copy.start()
    send_bwd(0)
    for k in (1, 3, 2):
        if k == 2:
            for copy in raw_z[1] + relays:
                copy.wait_recv()
        normalize(zx.at[k - 1], normed)
        dispatch_fwd(k, ztab.at[k - 1])
    own_f = [
        pltpu.make_async_copy(sent_f.at[e * 4], got_f.at[e, 0], own_sem.at[3, e]) for e in range(2)
    ]
    for copy in own_f:
        copy.start()
    for slot in (2, 3, 1):
        for e in range(2):
            send_fwd(e, slot).start()
    for r in (1, 3, 2):
        for copy in raw_x[r - 1]:
            copy.wait_recv()
        normalize(mx.at[r - 1], normed)
        dispatch_bwd(r, mtab.at[r - 1], mc.at[r - 1])
        send_bwd(r)
    for copy in weights + own_f:
        copy.wait()

    def forward(a):
        for e in range(2):
            for slot in (2 * a, 2 * a + 1):
                if slot:
                    send_fwd(e, slot).wait_recv()
        for e in range(2):
            forward_piece(a, e)
            for slot in (2 * a, 2 * a + 1):
                if slot:
                    return_fwd(e, slot).start()

    def backward(r):
        landed(got_h.at[rest(r)], hs_sem.at[r], hr_sem.at[r]).wait_recv()
        landed(got_c.at[rest(r)], cs_sem.at[r], cr_sem.at[r]).wait_recv()
        pltpu.make_async_copy(all_of(sent_h, r), all_of(got_h, r), own_sem.at[0, r]).wait()
        pltpu.make_async_copy(all_of(sent_c, r), all_of(got_c, r), own_sem.at[1, r]).wait()
        backward_chain(r)
        return_bwd(r)

    forward(0)
    backward(0)
    backward(1)
    forward(1)
    home = [
        pltpu.make_async_copy(out_f.at[e, 0], back_f.at[e * 4], own_sem.at[3, e]) for e in range(2)
    ]
    for copy in home:
        copy.start()
    backward(3)
    backward(2)
    strips(hid, got_c, units // TILE, grad_dn, 1)

    def returned(r):
        return landed(back_dh.at[rest(r)], es_sem.at[r], er_sem.at[r])

    def gathered_bwd(r, cols):
        return dot(pick_b[r].T, back_dh[pl.ds(r * PIECE, PIECE), cols])

    def home_bwd(r):
        returned(r).wait_recv()
        pltpu.make_async_copy(all_of(out_dh, r), all_of(back_dh, r), own_sem.at[2, r]).wait()

    back_x = []
    for r in (1, 3, 2):
        home_bwd(r)

        def sum_block(cols):
            mx[r - 1, :, cols] = gathered_bwd(r, cols).astype(bf16)

        wide(sum_block)
        copy = remote(
            mx.at[r - 1], sums_b.at[r - 1], ps_sem.at[r - 1], pr_sem.at[r - 1],
            peer(0, r % 2, 0, r // 2),
        )
        copy.start()
        back_x.append(copy)

    for e in range(2):
        for slot in (1, 2, 3):
            return_fwd(e, slot).wait_recv()
    for copy in home:
        copy.wait()

    def gated_rows(b, table):
        gates = slot_gates(table[1], pick_f.at[b])
        rows = back_f[:, b].reshape(PIECE, width).astype(f32) * gates
        lhs = rows.astype(bf16)
        back_f[:, b] = lhs.reshape(8, CAP, width)

    def gathered_fwd(b, cols):
        return dot(pick_f[b].T, back_f[:, b, :, cols].reshape(PIECE, WIDE))

    for copy in relays:
        copy.wait_send()
    back_z = []
    for b in (2, 1, 3):
        gated_rows(b, ztab.at[b - 1])

        def sum_rows(cols):
            zx[b - 1, :, cols] = gathered_fwd(b, cols).astype(bf16)

        wide(sum_rows)
        copy = remote(
            zx.at[b - 1], sums_f.at[b - 1], qs_sem.at[b - 1], qr_sem.at[b - 1], peer(-b, 0, 0, 0)
        )
        copy.start()
        back_z.append(copy)
    gated_rows(0, tab_f.at[0])

    strips(got_h, dboth, width // TILE, grad_gu, 0)

    home_bwd(0)

    def own_dh(cols):
        total[:, cols] = gathered_bwd(0, cols)

    wide(own_dh)
    for copy in back_z:
        copy.wait_recv()

    def own_y(cols):
        y = gathered_fwd(0, cols)
        for i in range(3):
            y = y + sums_f[i, :, cols].astype(f32)
        y_out[:, cols] = y.astype(bf16)

    wide(own_y)
    for copy in back_x:
        copy.wait_recv()

    def finish(i):
        rows = pl.ds(pl.multiple_of(i * 32, 32), 32)
        v = x_b[rows, :].astype(f32)
        scale = lax.rsqrt(jnp.mean(v * v, axis=-1, keepdims=True) + norm_eps)
        hat = v * scale
        dh = total[rows, :]
        for n in range(3):
            dh = dh + sums_b[n, rows, :].astype(f32)
        q = gain[...][None, :] * dh
        dx = scale * (q - hat * jnp.mean(hat * q, axis=-1, keepdims=True))
        dx_out[rows, :] = dx.astype(bf16)

    loop(x_b.shape[0] // 32, finish)

    for copies in raw_z + raw_x:
        for copy in copies:
            copy.wait_send()
    for copy in back_x + back_z:
        copy.wait_send()
    for e in range(2):
        for slot in (1, 2, 3):
            send_fwd(e, slot).wait_send()
            return_fwd(e, slot).wait_send()
    for r in range(4):
        landed(got_h.at[rest(r)], hs_sem.at[r], hr_sem.at[r]).wait_send()
        landed(got_c.at[rest(r)], cs_sem.at[r], cr_sem.at[r]).wait_send()
        returned(r).wait_send()


def writer(*refs):
    sems = refs[-1]
    held = refs[8:-1]
    reads, writes = [], []
    for n in range(4):
        src, dst, buf = refs[n], refs[4 + n], held[n]
        for at in range(0, src.shape[0], TILE):
            rows = pl.ds(at, min(TILE, src.shape[0] - at))
            i = len(reads)
            reads.append(pltpu.make_async_copy(src.at[rows], buf.at[rows], sems.at[0, i]))
            writes.append(pltpu.make_async_copy(buf.at[rows], dst.at[rows], sems.at[1, i]))
    for copy in reads:
        copy.start()
    for read, write in zip(reads, writes):
        read.wait()
        write.start()
    for copy in writes:
        copy.wait()


def per_device(
    x_fwd, gate_fwd, route_fwd, x_bwd, gate_bwd, route_bwd, cotangent, norm_gain, w_gate_up, w_down
):
    tokens, width = x_fwd.shape
    units = w_down.shape[2]

    rows = 32 * CAP
    anywhere = pl.BlockSpec(memory_space=pl.ANY)
    vmem = pl.BlockSpec(memory_space=pltpu.VMEM)
    dma = pltpu.SemaphoreType.DMA

    def hold(*shape, dtype=bf16):
        return pltpu.VMEM(shape, dtype)

    results = pl.pallas_call(
        kernel,
        out_shape=(
            jax.ShapeDtypeStruct((tokens, width), bf16),
            jax.ShapeDtypeStruct((tokens, width), bf16),
            jax.ShapeDtypeStruct((width, width), bf16),
            jax.ShapeDtypeStruct((units, width), bf16),
        ),
        in_specs=[vmem] * 8 + [anywhere] * 2,
        out_specs=(vmem, vmem, anywhere, anywhere),
        scratch_shapes=[
            hold(4, 2, 8, tokens, dtype=f32),
            hold(4, 2, 8, tokens, dtype=f32),
            hold(3, tokens, width),
            hold(3, 2, 8, tokens, dtype=f32),
            hold(3, tokens, width),
            hold(3, tokens, width),
            hold(3, 2, 8, tokens, dtype=f32),
            hold(tokens, width),
            hold(4, PIECE, tokens),
            hold(4, PIECE, tokens),
            hold(8, 4, CAP, width),
            hold(rows, width),
            hold(rows, width),
            hold(2, 4, 4, CAP, width),
            hold(rows, width),
            hold(rows, width),
            hold(2, width, width),
            hold(2, units, width),
            hold(2, 4, 4, CAP, width),
            hold(rows, width),
            hold(8, 4, CAP, width),
            hold(rows, width),
            hold(PIECE, units),
            hold(rows, units),
            hold(rows, width),
            hold(TILE, rows),
            hold(2, TILE, width),
            hold(3, tokens, width),
            hold(3, tokens, width),
            hold(tokens, width, dtype=f32),
            dma((2,)), dma((4, 4)), dma((2,)), dma((2,)), dma((2, 3)), dma((2, 3)), dma((3, 3)), dma((3, 3)),
            dma((2, 3)), dma((2, 3)), dma((4,)), dma((4,)), dma((4,)), dma((4,)),
            dma((2, 3)), dma((2, 3)), dma((4,)), dma((4,)), dma((3,)), dma((3,)),
            dma((3,)), dma((3,)), dma((2,)),
        ],
        compiler_params=pltpu.CompilerParams(
            collective_id=0, has_side_effects=True, vmem_limit_bytes=67043328
        ),
    )(
        x_fwd,
        x_bwd,
        cotangent,
        norm_gain,
        route_fwd.T,
        gate_fwd.T,
        route_bwd.T,
        gate_bwd.T,
        w_gate_up[0],
        w_down[0],
    )
    y_fwd, dx_bwd, grad_gu, grad_dn = pl.pallas_call(
        writer,
        out_shape=tuple(jax.ShapeDtypeStruct(r.shape, r.dtype) for r in results),
        in_specs=[anywhere] * 4,
        out_specs=(anywhere,) * 4,
        scratch_shapes=[hold(*r.shape) for r in results] + [dma((2, 11))],
        compiler_params=pltpu.CompilerParams(vmem_limit_bytes=67043328),
    )(*results)
    return y_fwd, dx_bwd, grad_gu[None, None], grad_dn[None, None]


def solution(mesh):
    rows = P(("pipe", "expert"), None)
    weights = P("pipe", "expert", None, None)
    return jax.shard_map(
        per_device,
        mesh=mesh,
        in_specs=(rows,) * 7 + (P(), weights, weights),
        out_specs=(rows, rows, weights, weights),
        check_vma=False,
    )
```

```python
import jax
import jax.numpy as jnp
from jax import lax
from jax.experimental import pallas as pl
from jax.experimental.pallas import tpu as pltpu
from jax.sharding import PartitionSpec as P

norm_eps = 1e-06
bf16 = jnp.bfloat16
f32 = jnp.float32
MESH = pl.DeviceIdType.MESH
CAP = 32
TILE = 256
WIDE = 512
PIECE = 8 * CAP
NT = (((1,), (1,)), ((), ()))


def place():
    p, d = lax.axis_index("pipe"), lax.axis_index("expert")
    return p, p // 4, d // 4, (d // 2) % 2, d % 2


def peer(kz, kx, kc, kh):
    p, _, z, xl, c = place()
    return p + kh * (7 - 2 * p), ((z + kz + 4) % 4) * 4 + ((xl + kx) % 2) * 2 + (c + kc) % 2


def dot(a, b):
    return jnp.dot(a, b, preferred_element_type=f32)


def dot_nt(a, b):
    return lax.dot_general(a, b, NT, preferred_element_type=f32)


def loop(count, body):
    def step(i, _):
        body(i)
        return 0

    lax.fori_loop(0, count, step, 0)


def kernel(
    x_f, x_b, cot, gain, routes_f, gates_f, routes_b, gates_b, w_gu, w_dn,
    y_out, dx_out, grad_gu, grad_dn,
    tab_f, tab_b, zx, ztab, mx, mc, mtab, normed, pick_f, pick_b, sent_f, sent_h, sent_c, got_f, got_h, got_c,
    gu, dn, out_f, out_dh, back_f, back_dh, hid_f, hid, dboth, lhs_t, gout, sums_f, sums_b, total,
    w_sem, own_sem, rs_sem, rr_sem, zs_sem, zr_sem, ms_sem, mr_sem, fs_sem, fr_sem, hs_sem, hr_sem, cs_sem, cr_sem,
    ds_sem, dr_sem, es_sem, er_sem, qs_sem, qr_sem, ps_sem, pr_sem, g_sem,
):
    width = got_h.shape[1]
    units = dn.shape[1]
    half = place()[1]
    here = peer(0, 0, 0, 0)

    def remote(src, dst, ssem, rsem, to):
        return pltpu.make_async_remote_copy(
            src_ref=src, dst_ref=dst, send_sem=ssem, recv_sem=rsem, device_id=to, device_id_type=MESH
        )

    def landed(dst, ssem, rsem):
        return remote(dst, dst, ssem, rsem, here)

    barrier = pltpu.get_barrier_semaphore()
    others = [(kz, 0, kc, 0) for kc in range(2) for kz in range(4)][1:]
    others += [(0, 1, 0, 0), (0, 1, 1, 0), (0, 0, 0, 1), (0, 1, 0, 1)]
    for other in others:
        pl.semaphore_signal(barrier, inc=1, device_id=peer(*other), device_id_type=MESH)

    weights = [
        pltpu.make_async_copy(w_gu, gu, w_sem.at[0]),
        pltpu.make_async_copy(w_dn, dn, w_sem.at[1]),
    ]
    for copy in weights:
        copy.start()

    def normalize(src, dst):
        def some(i):
            rows = pl.ds(pl.multiple_of(i * 32, 32), 32)
            v = src[rows, :].astype(f32)
            scale = lax.rsqrt(jnp.mean(v * v, axis=-1, keepdims=True) + norm_eps)
            dst[rows, :] = (v * scale * gain[...][None, :]).astype(bf16)

        loop(src.shape[0] // 32, some)

    def tables(routes, gates, experts, dst):
        chosen = jnp.zeros((32, 128), f32)
        weight = jnp.zeros((32, 128), f32)
        for n in range(routes.shape[0]):
            hit = routes[n : n + 1, :] == experts
            chosen = jnp.where(hit, 1.0, chosen)
            weight = jnp.where(hit, gates[n : n + 1, :], weight)
        row = lax.broadcasted_iota(jnp.int32, (128, 128), 0)
        col = lax.broadcasted_iota(jnp.int32, (128, 128), 1)
        earlier = jnp.where(row < col, 1.0, 0.0).astype(bf16)
        slots = jnp.where(chosen > 0.0, dot(chosen.astype(bf16), earlier), -1.0)
        dst[:, 0] = slots.reshape(4, 8, 128)
        dst[:, 1] = weight.reshape(4, 8, 128)

    def picks(slots, dst):
        want = lax.broadcasted_iota(jnp.int32, (8, CAP, 128), 1).astype(f32)
        hit = jnp.where(slots[:, None, :] == want, 1.0, 0.0).reshape(PIECE, 128)
        dst[...] = hit.astype(bf16)

    def slot_gates(gates, pick):
        each = jnp.broadcast_to(gates[:, None, :], (8, CAP, 128)).reshape(PIECE, 128)
        return jnp.sum(pick[...].astype(f32) * each, axis=1, keepdims=True)

    def wide(body):
        loop(width // WIDE, lambda t: body(pl.ds(pl.multiple_of(t * WIDE, WIDE), WIDE)))

    def over_z(k):
        table = remote(
            tab_f.at[k], ztab.at[k - 1], zs_sem.at[1, k - 1], zr_sem.at[1, k - 1], peer(k, 0, 0, 0)
        )
        if k == 2:
            return [table]
        rows = remote(
            x_f, zx.at[k - 1], zs_sem.at[0, k - 1], zr_sem.at[0, k - 1], peer(k, 0, 0, 0)
        )
        return [table, rows]

    def relay(k):
        part = pl.ds(0 if k == 1 else 64, 64)
        i = k // 2
        return remote(
            zx.at[k - 1, part], zx.at[1, part], rs_sem.at[i], rr_sem.at[i], peer(k, 0, 0, 0)
        )

    def over_x(r):
        to = peer(0, r % 2, 0, r // 2)
        i = r - 1
        return [
            remote(x_b, mx.at[i], ms_sem.at[0, i], mr_sem.at[0, i], to),
            remote(cot, mc.at[i], ms_sem.at[1, i], mr_sem.at[1, i], to),
            remote(tab_b.at[r], mtab.at[i], ms_sem.at[2, i], mr_sem.at[2, i], to),
        ]

    raw_z = [over_z(k) for k in (1, 2, 3)]
    raw_x = [over_x(r) for r in (1, 2, 3)]
    relays = [relay(1), relay(3)]

    def send_fwd(e, slot):
        return remote(
            sent_f.at[e * 4 + slot], got_f.at[e, slot], fs_sem.at[e, slot - 1], fr_sem.at[e, slot - 1],
            peer(0, slot // 2, slot % 2, 0),
        )

    def return_fwd(e, slot):
        return remote(
            out_f.at[e, slot], back_f.at[e * 4 + slot], ds_sem.at[e, slot - 1],
            dr_sem.at[e, slot - 1], peer(0, slot // 2, slot % 2, 0),
        )

    def send_bwd(r):
        def go(j, _):
            to = peer(j % 4, 0, j // 4, 0)
            rows = pl.ds(r * PIECE + j * CAP, CAP)
            remote(sent_h.at[rows], got_h.at[rows], hs_sem.at[r], hr_sem.at[r], to).start()
            remote(sent_c.at[rows], got_c.at[rows], cs_sem.at[r], cr_sem.at[r], to).start()
            return 0

        lax.fori_loop(1, 8, go, 0)
        first = pl.ds(r * PIECE, CAP)
        pltpu.make_async_copy(sent_h.at[first], got_h.at[first], own_sem.at[0, r]).start()
        pltpu.make_async_copy(sent_c.at[first], got_c.at[first], own_sem.at[1, r]).start()

    def return_bwd(r):
        def go(j, _):
            to = peer(-(j % 4), 0, j // 4, 0)
            rows = pl.ds(r * PIECE + j * CAP, CAP)
            remote(out_dh.at[rows], back_dh.at[rows], es_sem.at[r], er_sem.at[r], to).start()
            return 0

        lax.fori_loop(1, 8, go, 0)
        first = pl.ds(r * PIECE, CAP)
        pltpu.make_async_copy(out_dh.at[first], back_dh.at[first], own_sem.at[2, r]).start()

    def rest(r):
        return pl.ds(r * PIECE + CAP, PIECE - CAP)

    def all_of(ref, r):
        return ref.at[pl.ds(r * PIECE, CAP)]

    def forward_piece(a, e):
        def first(t):
            at = pl.multiple_of(t * TILE, TILE)
            x = got_f[e, 2 * a : 2 * a + 2].reshape(PIECE, width)
            gate = dot(x, gu[e, :, pl.ds(at, TILE)])
            up = dot(x, gu[e, :, pl.ds(units + at, TILE)])
            hid_f[:, pl.ds(at, TILE)] = (gate * jax.nn.sigmoid(gate) * up).astype(bf16)

        loop(units // TILE, first)

        def second(t):
            cols = pl.ds(pl.multiple_of(t * TILE, TILE), TILE)
            rows = dot(hid_f[...], dn[e, :, cols]).astype(bf16)
            out_f[e, 2 * a : 2 * a + 2, :, :, cols] = rows.reshape(2, 4, CAP, TILE)

        loop(width // TILE, second)

    def backward_chain(r):
        rows = pl.ds(r * PIECE, PIECE)

        def first(t):
            at = pl.multiple_of(t * TILE, TILE)
            cols = pl.ds(at, TILE)
            more = pl.ds(units + at, TILE)
            x = got_h[rows, :]
            gate = dot(x, gu[half, :, cols])
            up = dot(x, gu[half, :, more])
            back = dot_nt(got_c[rows, :], dn[half, cols, :])
            squash = jax.nn.sigmoid(gate)
            active = gate * squash
            hid[rows, cols] = (active * up).astype(bf16)
            dboth[rows, cols] = (back * up * squash * (1.0 + gate * (1.0 - squash))).astype(bf16)
            dboth[rows, more] = (back * active).astype(bf16)

        loop(units // TILE, first)

        def second(t):
            cols = pl.ds(pl.multiple_of(t * TILE, TILE), TILE)
            out_dh[rows, cols] = dot_nt(dboth[rows, :], gu[half, cols, :]).astype(bf16)

        loop(width // TILE, second)

    def strips(lhs, rhs, which, dst):
        copies = []
        for n, m in enumerate(which):
            rows = pl.ds(m * TILE, TILE)
            buf = n % 2
            lhs_t[...] = lhs[:, rows].T
            if n >= 2:
                copies[n - 2].wait()

            def cols_of(t):
                cols = pl.ds(pl.multiple_of(t * TILE, TILE), TILE)
                gout[buf, :, cols] = dot(lhs_t[...], rhs[:, cols]).astype(bf16)

            loop(width // TILE, cols_of)
            copies.append(pltpu.make_async_copy(gout.at[buf], dst.at[rows], g_sem.at[buf]))
            copies[n].start()
        for copy in copies[-2:]:
            copy.wait()

    def dispatch_fwd(b, table):
        picks(table[0], pick_f.at[b])

        def some(cols):
            rows = dot(pick_f[b], normed[:, cols]).astype(bf16)
            sent_f[:, b, :, cols] = rows.reshape(8, CAP, WIDE)

        wide(some)

    def dispatch_bwd(r, table, c_rows):
        picks(table[0], pick_b.at[r])
        gates = slot_gates(table[1], pick_b.at[r])
        rows = pl.ds(r * PIECE, PIECE)

        def some(cols):
            sent_h[rows, cols] = dot(pick_b[r], normed[:, cols]).astype(bf16)
            sent_c[rows, cols] = (dot(pick_b[r], c_rows[:, cols]) * gates).astype(bf16)

        wide(some)

    _, _, z, xl, c = place()
    k = lax.broadcasted_iota(jnp.int32, (32, 128), 0)
    agent, s = k >> 3, k & 7
    d_f = ((z + agent) & 3) * 4 + ((xl + (s >> 1)) & 1) * 2 + ((c + s) & 1)
    d_b = ((z + s) & 3) * 4 + ((xl + agent) & 1) * 2 + ((c + (s >> 2)) & 1)
    tables(routes_f, gates_f, 2 * d_f + (s >> 2), tab_f)
    tables(routes_b, gates_b, 2 * d_b + ((half + (agent >> 1)) & 1), tab_b)
    normalize(x_b, normed)
    pl.semaphore_wait(barrier, len(others))
    for copies in raw_z + [raw_x[0], raw_x[2], raw_x[1]]:
        for copy in copies:
            copy.start()
    dispatch_bwd(0, tab_b.at[0], cot)

    normalize(x_f, normed)
    dispatch_fwd(0, tab_f.at[0])
    for k, copy in zip((1, 3), relays):
        for raw in raw_z[k - 1]:
            raw.wait_recv()
        copy.start()
    send_bwd(0)
    for k in (1, 3, 2):
        if k == 2:
            for copy in raw_z[1] + relays:
                copy.wait_recv()
        normalize(zx.at[k - 1], normed)
        dispatch_fwd(k, ztab.at[k - 1])
    own_f = [
        pltpu.make_async_copy(sent_f.at[e * 4], got_f.at[e, 0], own_sem.at[3, e]) for e in range(2)
    ]
    for copy in own_f:
        copy.start()
    for slot in (2, 3, 1):
        for e in range(2):
            send_fwd(e, slot).start()
    for r in (1, 3, 2):
        for copy in raw_x[r - 1]:
            copy.wait_recv()
        normalize(mx.at[r - 1], normed)
        dispatch_bwd(r, mtab.at[r - 1], mc.at[r - 1])
        send_bwd(r)
    for copy in weights + own_f:
        copy.wait()

    def forward(a):
        for e in range(2):
            for slot in (2 * a, 2 * a + 1):
                if slot:
                    send_fwd(e, slot).wait_recv()
        for e in range(2):
            forward_piece(a, e)
            for slot in (2 * a, 2 * a + 1):
                if slot:
                    return_fwd(e, slot).start()

    def backward(r):
        landed(got_h.at[rest(r)], hs_sem.at[r], hr_sem.at[r]).wait_recv()
        landed(got_c.at[rest(r)], cs_sem.at[r], cr_sem.at[r]).wait_recv()
        pltpu.make_async_copy(all_of(sent_h, r), all_of(got_h, r), own_sem.at[0, r]).wait()
        pltpu.make_async_copy(all_of(sent_c, r), all_of(got_c, r), own_sem.at[1, r]).wait()
        backward_chain(r)
        return_bwd(r)

    forward(0)
    backward(1)
    forward(1)
    home = [
        pltpu.make_async_copy(out_f.at[e, 0], back_f.at[e * 4], own_sem.at[3, e]) for e in range(2)
    ]
    for copy in home:
        copy.start()
    backward(3)
    backward(2)
    backward(0)
    strips(hid, got_c, range(units // TILE), grad_dn)

    def returned(r):
        return landed(back_dh.at[rest(r)], es_sem.at[r], er_sem.at[r])

    def gathered_bwd(r, cols):
        return dot(pick_b[r].T, back_dh[pl.ds(r * PIECE, PIECE), cols])

    def home_bwd(r):
        returned(r).wait_recv()
        pltpu.make_async_copy(all_of(out_dh, r), all_of(back_dh, r), own_sem.at[2, r]).wait()

    back_x = []
    for r in (1, 3, 2):
        home_bwd(r)

        def sum_block(cols):
            mx[r - 1, :, cols] = gathered_bwd(r, cols).astype(bf16)

        wide(sum_block)
        copy = remote(
            mx.at[r - 1], sums_b.at[r - 1], ps_sem.at[r - 1], pr_sem.at[r - 1],
            peer(0, r % 2, 0, r // 2),
        )
        copy.start()
        back_x.append(copy)

    for e in range(2):
        for slot in (1, 2, 3):
            return_fwd(e, slot).wait_recv()
    for copy in home:
        copy.wait()

    def gated_rows(b, table):
        gates = slot_gates(table[1], pick_f.at[b])
        rows = back_f[:, b].reshape(PIECE, width).astype(f32) * gates
        lhs = rows.astype(bf16)
        back_f[:, b] = lhs.reshape(8, CAP, width)

    def gathered_fwd(b, cols):
        return dot(pick_f[b].T, back_f[:, b, :, cols].reshape(PIECE, WIDE))

    for copy in relays:
        copy.wait_send()
    back_z = []
    for b in (2, 1, 3):
        gated_rows(b, ztab.at[b - 1])

        def sum_rows(cols):
            zx[b - 1, :, cols] = gathered_fwd(b, cols).astype(bf16)

        wide(sum_rows)
        copy = remote(
            zx.at[b - 1], sums_f.at[b - 1], qs_sem.at[b - 1], qr_sem.at[b - 1], peer(-b, 0, 0, 0)
        )
        copy.start()
        back_z.append(copy)
    gated_rows(0, tab_f.at[0])

    strips(got_h, dboth, range(width // TILE), grad_gu)

    home_bwd(0)

    def own_dh(cols):
        total[:, cols] = gathered_bwd(0, cols)

    wide(own_dh)
    for copy in back_z:
        copy.wait_recv()

    def own_y(cols):
        y = gathered_fwd(0, cols)
        for i in range(3):
            y = y + sums_f[i, :, cols].astype(f32)
        y_out[:, cols] = y.astype(bf16)

    wide(own_y)
    for copy in back_x:
        copy.wait_recv()

    def finish(i):
        rows = pl.ds(pl.multiple_of(i * 32, 32), 32)
        v = x_b[rows, :].astype(f32)
        scale = lax.rsqrt(jnp.mean(v * v, axis=-1, keepdims=True) + norm_eps)
        hat = v * scale
        dh = total[rows, :]
        for n in range(3):
            dh = dh + sums_b[n, rows, :].astype(f32)
        q = gain[...][None, :] * dh
        dx = scale * (q - hat * jnp.mean(hat * q, axis=-1, keepdims=True))
        dx_out[rows, :] = dx.astype(bf16)

    loop(x_b.shape[0] // 32, finish)

    for copies in raw_z + raw_x:
        for copy in copies:
            copy.wait_send()
    for copy in back_x + back_z:
        copy.wait_send()
    for e in range(2):
        for slot in (1, 2, 3):
            send_fwd(e, slot).wait_send()
            return_fwd(e, slot).wait_send()
    for r in range(4):
        landed(got_h.at[rest(r)], hs_sem.at[r], hr_sem.at[r]).wait_send()
        landed(got_c.at[rest(r)], cs_sem.at[r], cr_sem.at[r]).wait_send()
        returned(r).wait_send()


def writer(*refs):
    sems = refs[-1]
    held = refs[8:-1]
    reads, writes = [], []
    for n in range(4):
        src, dst, buf = refs[n], refs[4 + n], held[n]
        for at in range(0, src.shape[0], TILE):
            rows = pl.ds(at, min(TILE, src.shape[0] - at))
            i = len(reads)
            reads.append(pltpu.make_async_copy(src.at[rows], buf.at[rows], sems.at[0, i]))
            writes.append(pltpu.make_async_copy(buf.at[rows], dst.at[rows], sems.at[1, i]))
    for copy in reads:
        copy.start()
    for read, write in zip(reads, writes):
        read.wait()
        write.start()
    for copy in writes:
        copy.wait()


def per_device(
    x_fwd, gate_fwd, route_fwd, x_bwd, gate_bwd, route_bwd, cotangent, norm_gain, w_gate_up, w_down
):
    tokens, width = x_fwd.shape
    units = w_down.shape[2]

    rows = 32 * CAP
    anywhere = pl.BlockSpec(memory_space=pl.ANY)
    vmem = pl.BlockSpec(memory_space=pltpu.VMEM)
    dma = pltpu.SemaphoreType.DMA

    def hold(*shape, dtype=bf16):
        return pltpu.VMEM(shape, dtype)

    results = pl.pallas_call(
        kernel,
        out_shape=(
            jax.ShapeDtypeStruct((tokens, width), bf16),
            jax.ShapeDtypeStruct((tokens, width), bf16),
            jax.ShapeDtypeStruct((width, width), bf16),
            jax.ShapeDtypeStruct((units, width), bf16),
        ),
        in_specs=[vmem] * 8 + [anywhere] * 2,
        out_specs=(vmem, vmem, anywhere, anywhere),
        scratch_shapes=[
            hold(4, 2, 8, tokens, dtype=f32),
            hold(4, 2, 8, tokens, dtype=f32),
            hold(3, tokens, width),
            hold(3, 2, 8, tokens, dtype=f32),
            hold(3, tokens, width),
            hold(3, tokens, width),
            hold(3, 2, 8, tokens, dtype=f32),
            hold(tokens, width),
            hold(4, PIECE, tokens),
            hold(4, PIECE, tokens),
            hold(8, 4, CAP, width),
            hold(rows, width),
            hold(rows, width),
            hold(2, 4, 4, CAP, width),
            hold(rows, width),
            hold(rows, width),
            hold(2, width, width),
            hold(2, units, width),
            hold(2, 4, 4, CAP, width),
            hold(rows, width),
            hold(8, 4, CAP, width),
            hold(rows, width),
            hold(PIECE, units),
            hold(rows, units),
            hold(rows, width),
            hold(TILE, rows),
            hold(2, TILE, width),
            hold(3, tokens, width),
            hold(3, tokens, width),
            hold(tokens, width, dtype=f32),
            dma((2,)), dma((4, 4)), dma((2,)), dma((2,)), dma((2, 3)), dma((2, 3)), dma((3, 3)), dma((3, 3)),
            dma((2, 3)), dma((2, 3)), dma((4,)), dma((4,)), dma((4,)), dma((4,)),
            dma((2, 3)), dma((2, 3)), dma((4,)), dma((4,)), dma((3,)), dma((3,)),
            dma((3,)), dma((3,)), dma((2,)),
        ],
        compiler_params=pltpu.CompilerParams(
            collective_id=0, has_side_effects=True, vmem_limit_bytes=67043328
        ),
    )(
        x_fwd,
        x_bwd,
        cotangent,
        norm_gain,
        route_fwd.T,
        gate_fwd.T,
        route_bwd.T,
        gate_bwd.T,
        w_gate_up[0],
        w_down[0],
    )
    y_fwd, dx_bwd, grad_gu, grad_dn = pl.pallas_call(
        writer,
        out_shape=tuple(jax.ShapeDtypeStruct(r.shape, r.dtype) for r in results),
        in_specs=[anywhere] * 4,
        out_specs=(anywhere,) * 4,
        scratch_shapes=[hold(*r.shape) for r in results] + [dma((2, 11))],
        compiler_params=pltpu.CompilerParams(vmem_limit_bytes=67043328),
    )(*results)
    return y_fwd, dx_bwd, grad_gu[None, None], grad_dn[None, None]


def solution(mesh):
    rows = P(("pipe", "expert"), None)
    weights = P("pipe", "expert", None, None)
    return jax.shard_map(
        per_device,
        mesh=mesh,
        in_specs=(rows,) * 7 + (P(), weights, weights),
        out_specs=(rows, rows, weights, weights),
        check_vma=False,
    )
```
